32 devices in a mesh: tm: 16 (over z, y, core), strip: 2 (over x).
Axes of the slice: x: 2, y: 2, z: 4, core: 2. Of those that a mesh axis runs over, the one named last changes fastest.
Arguments:
- forward_u: float32 [16, 128, 1024], P('tm', 'strip'), may hold values from -4 to 4
- forward_v: float32 [16, 128, 1024], P('tm', 'strip'), may hold values from -4 to 4
- permittivity: float32 [128, 1024], P('strip'), may hold values from 1 to 3
- coarse_rate: float32 [16, 128, 1024], P('tm', 'strip'), may hold values from 0.2 to 8
- modulation: float32 [32], replicated, may hold values from 0 to 0.3
- tile_map: int32 [1, 8], replicated, may hold values from 0 to 31
- start_step: int32 [16], P('tm'), may hold values from 0 to 255
Outputs:
- adjoint_u: float32 [16, 128, 1024], P('tm', 'strip')
- adjoint_v: float32 [16, 128, 1024], P('tm', 'strip')
- depth_grad: float32 [32], replicated
The draws below stay inside these ranges and needn't reach their ends.
Inputs may be any that keep to these rules, and one draw needn't show every extreme that they name: `tile_map`: tile parameter indices. `start_step`: start steps within one period.
All inputs are finite; a program needn't handle non-finite values.
Results may differ from the reference program's by a relative error of at most 0.0003.
Values sent between devices are 32-bit elements; how exact they have to be, the bound alone decides.
A program may use at most 128 MiB of HBM per device.

```python
import math
import jax
import jax.numpy as jnp
from jax import lax

NY = 1024
TILE = 128
STEPS = 2
STENCIL = 4
PERIOD = 256
PARAMS = 32
SLICES = 16
NX = 128
TX = 1
TY = 8


def touch_ends(entries, rng, smallest, top_value):
    longest = entries.shape.index(max(entries.shape))
    spots = []
    for shift in (0, 1):
        where = [jax.random.randint(jax.random.fold_in(rng, axis), (), 0, length) for axis, length in enumerate(entries.shape)]
        where[longest] = (where[longest] + shift) % entries.shape[longest]
        spots.append(tuple(where))
    return entries.at[spots[0]].set(smallest).at[spots[1]].set(top_value)


def levels(rng, shape, pieces, smallest, largest):
    def one(axis_at, parts):
        steps = jax.random.uniform(jax.random.fold_in(jax.random.fold_in(rng, 6), axis_at), (parts,), jnp.float32, smallest / len(pieces), largest / len(pieces))
        return jnp.repeat(jnp.exp(steps), shape[axis_at] // parts).reshape((-1,) + (1,) * (len(shape) - axis_at - 1))

    loudness = one(*pieces[0])
    for cut in pieces[1:]:
        loudness = loudness * one(*cut)
    return loudness


def centred(key, extent, spread, reach, split=(), held_as=jnp.bfloat16):
    entries = jax.random.normal(key, extent, jnp.float32) * spread
    if len(split) > 0:
        entries = levels(key, extent, split, -0.22, 0.18) * entries
    return jnp.clip(entries, min=-reach, max=reach).astype(held_as)


def setup_inputs(seed: int = 0) -> dict:
    seeds = jax.random.split(jax.random.key(seed), 8)
    forward_u = centred(seeds[0], (SLICES, NX, NY), 0.5, 4.0, ((0, 16), (1, 2)), jnp.float32)
    forward_v = centred(seeds[1], (SLICES, NX, NY), 0.5, 4.0, ((0, 16), (1, 2)), jnp.float32)
    permittivity = jnp.clip(1.0 + 2.0 * jax.random.uniform(seeds[2], (NX, NY), jnp.float32) ** levels(seeds[2], (NX, NY), ((0, 2),), -0.2, 0.2), 1.0, 3.0)
    coarse_rate = jnp.clip(jnp.exp(math.log(8.0) - 3.6888794 * jax.random.uniform(seeds[3], (SLICES, NX, NY), jnp.float32) ** levels(seeds[3], (SLICES, NX, NY), ((0, 16), (1, 2)), -0.2, 0.2)), 0.2, 8.0)
    modulation = jnp.clip(jax.random.uniform(seeds[4], (PARAMS,), jnp.float32, 0.0, 0.3), 0.0, 0.3)
    tile_map = touch_ends(jax.random.randint(seeds[5], (TX, TY), 0, PARAMS), jax.random.fold_in(seeds[5], 1), 0, PARAMS - 1).astype(jnp.int32)
    start_step = touch_ends(jax.random.randint(seeds[6], (SLICES,), 0, PERIOD), jax.random.fold_in(seeds[6], 1), 0, PERIOD - 1).astype(jnp.int32)
    return dict(forward_u=forward_u, forward_v=forward_v, permittivity=permittivity, coarse_rate=coarse_rate, modulation=modulation, tile_map=tile_map, start_step=start_step)


stencil_coef = (-205.0 / 72.0, 8.0 / 5.0, -1.0 / 5.0, 8.0 / 315.0, -1.0 / 560.0)
time_step = 0.4
damping_rate = 0.1


def laplacian_rows(padded, rim_width):
    row_count = padded.shape[0] - 2 * rim_width
    center = padded[rim_width:rim_width + row_count]
    summed = (2.0 * stencil_coef[0]) * center
    for offset in range(1, 5):
        along_x = padded[rim_width + offset:rim_width + offset + row_count] + padded[rim_width - offset:rim_width - offset + row_count]
        along_y = jnp.roll(center, offset, axis=1) + jnp.roll(center, -offset, axis=1)
        summed = summed + stencil_coef[offset] * (along_x + along_y)
    return summed


def pad_rows(field):
    return jnp.pad(field, ((STENCIL, STENCIL), (0, 0)))


def reference(forward_u, forward_v, permittivity, coarse_rate, modulation, tile_map, start_step):
    cell_depth = jnp.repeat(jnp.repeat(modulation[tile_map], TILE, axis=0), TILE, axis=1)

    def phases(start_index):
        offsets = (start_index + jnp.arange(STEPS, dtype=jnp.int32)).astype(jnp.float32)
        return jnp.cos((2.0 * jnp.pi / PERIOD) * offsets)

    def forward_run(field_u, field_v, cosines):
        forcings = []
        eps_all = []
        for level in range(STEPS):
            eps_now = permittivity * (1.0 + cell_depth * cosines[level])
            forcing = laplacian_rows(pad_rows(field_u), STENCIL) - damping_rate * field_v
            forcings.append(forcing)
            eps_all.append(eps_now)
            field_v = field_v + time_step * forcing / eps_now
            field_u = field_u + time_step * field_v
        return field_u, field_v, forcings, eps_all

    def forward_map(element):
        field_u, field_v, start_index = element
        end_u, end_v, forcings, eps_all = forward_run(field_u, field_v, phases(start_index))
        return end_u, end_v

    end_u, end_v = lax.map(forward_map, (forward_u, forward_v, start_step))
    mismatch_u = end_u - jnp.roll(forward_u, -1, axis=0)
    mismatch_v = end_v - jnp.roll(forward_v, -1, axis=0)
    retain = jnp.exp(-coarse_rate / SLICES)

    def compose(carried, element):
        cycle_a, cycle_bu, cycle_bv = carried
        factor, term_u, term_v = element
        return (factor * cycle_a, factor * cycle_bu + term_u, factor * cycle_bv + term_v), None

    ones = jnp.ones((NX, NY), jnp.float32)
    zeros = jnp.zeros((NX, NY), jnp.float32)
    (cycle_a, cycle_bu, cycle_bv), unused = lax.scan(compose, (ones, zeros, zeros), (retain, mismatch_u, mismatch_v), reverse=True)
    first_u = cycle_bu / (1.0 - cycle_a)
    first_v = cycle_bv / (1.0 - cycle_a)

    def backward(carried, element):
        factor, term_u, term_v = element
        coarse_u = factor * carried[0] + term_u
        coarse_v = factor * carried[1] + term_v
        return (coarse_u, coarse_v), (coarse_u, coarse_v)

    unused, (coarse_u, coarse_v) = lax.scan(backward, (first_u, first_v), (retain, mismatch_u, mismatch_v), reverse=True)

    def adjoint_map(element):
        field_u, field_v, back_u, back_v, start_index = element
        cosines = phases(start_index)
        end_u, end_v, forcings, eps_all = forward_run(field_u, field_v, cosines)
        gradient_cells = jnp.zeros((NX, NY), jnp.float32)
        for level in reversed(range(STEPS)):
            eps_now = eps_all[level]
            total_v = back_v + time_step * back_u
            weighted = (time_step / eps_now) * total_v
            back_u = back_u + laplacian_rows(pad_rows(weighted), STENCIL)
            back_v = (1.0 - time_step * damping_rate / eps_now) * total_v
            gradient_cells = gradient_cells - cosines[level] * time_step * total_v * forcings[level] / (eps_now * eps_now)
        cell_terms = gradient_cells * permittivity
        tile_sums = jnp.sum(cell_terms.reshape(NX // TILE, TILE, NY // TILE, TILE), axis=(1, 3))
        return back_u, back_v, tile_sums

    back_u, back_v, tile_sums = lax.map(adjoint_map, (forward_u, forward_v, coarse_u, coarse_v, start_step))
    adjoint_u = back_u - jnp.roll(coarse_u, 1, axis=0)
    adjoint_v = back_v - jnp.roll(coarse_v, 1, axis=0)
    tile_total = jnp.sum(tile_sums, axis=0)
    depth_grad = jax.ops.segment_sum(tile_total.reshape(-1), tile_map.reshape(-1).astype(jnp.int32), num_segments=PARAMS)
    return adjoint_u, adjoint_v, depth_grad
```

```python
import functools

import jax
import jax.numpy as jnp
from jax import lax
from jax.experimental import pallas as pl
from jax.experimental.pallas import tpu as pltpu
from jax.sharding import PartitionSpec as P

TILE = 128
STEPS = 2
STENCIL = 4
PERIOD = 256
RIM = STEPS * STENCIL
BASE = 2 * RIM

stencil_coef = (-205.0 / 72.0, 8.0 / 5.0, -1.0 / 5.0, 8.0 / 315.0, -1.0 / 560.0)
time_step = 0.4
damping_rate = 0.1

MESH = pl.DeviceIdType.MESH


def laplacian(ref, base):
    center = ref[base : base + 8, :]
    cols = center.shape[1]
    summed = (2.0 * stencil_coef[0]) * center
    for o in range(1, STENCIL + 1):
        along_x = ref[base + o : base + o + 8, :] + ref[base - o : base - o + 8, :]
        along_y = pltpu.roll(center, o, 1) + pltpu.roll(center, cols - o, 1)
        summed = summed + stencil_coef[o] * (along_x + along_y)
    return summed


def kernel(
    n, S, tile_rows,
    u_in, v_in, p_in, rate_in, mod, tmap, step0,
    out_u, out_v, out_g,
    Ub, Vb, Pb, Q, Fo, U1, Cb, W1, B1, W0, Fn, ends, Rown, Rpar, Am, Mp, E, RA, RE, X, G, Cx, Pre,
    part, gat1, gat2,
    load_sem, halo_s, halo_r, shift_s, shift_r, rate_s, rate_r, a_s, a_r, m_s, m_r, e_s, e_r,
    g_s, g_r, c_s, c_r, h_s, h_r, p_s, p_r, d1_s, d1_r, d2_s, d2_r,
):
    k = lax.axis_index("tm")
    s = lax.axis_index("strip")
    nc = n // 2
    c = k // 2
    j = k % 2
    partner = 2 * c + 1 - j
    R, C = out_u.shape
    H = R // 2
    W = H * C // (8 * nc)
    cpr = C // W

    def chip(d):
        return 2 * lax.rem(c + d + nc, nc) + j

    mine = pl.ds(pl.multiple_of(j * H, 8), H)
    other = pl.ds(pl.multiple_of((1 - j) * H, 8), H)
    loads = [
        pltpu.make_async_copy(u_in, Ub.at[pl.ds(BASE, R)], load_sem.at[0]),
        pltpu.make_async_copy(v_in, Vb.at[pl.ds(BASE, R)], load_sem.at[1]),
        pltpu.make_async_copy(p_in, Pb.at[pl.ds(BASE, R)], load_sem.at[2]),
        pltpu.make_async_copy(rate_in.at[mine], Rown, load_sem.at[3]),
    ]
    for load in loads:
        load.start()

    barrier = pltpu.get_barrier_semaphore()
    for d in range(1, nc):
        pl.semaphore_signal(barrier, inc=1, device_id=(chip(d), s), device_id_type=MESH)
    for d in range(1, 2 * S):
        at = lax.rem(s * 2 + j + d, 2 * S)
        pl.semaphore_signal(
            barrier, inc=1, device_id=(2 * c + at % 2, at // 2), device_id_type=MESH
        )
    aside = lax.rem(k + 2 * j - 1 + n, n)
    pl.semaphore_signal(barrier, inc=1, device_id=(aside, s), device_id_type=MESH)
    pl.semaphore_wait(barrier, (nc - 1) + (2 * S - 1) + 1)

    def remote(src, dst, ss, rs, where):
        return pltpu.make_async_remote_copy(
            src_ref=src, dst_ref=dst, send_sem=ss, recv_sem=rs,
            device_id=where, device_id_type=MESH,
        )

    up = lax.rem(s + S - 1, S)
    down = lax.rem(s + 1, S)
    tops = pl.ds(BASE - RIM, RIM)
    bottoms = pl.ds(BASE + R, RIM)
    has_up = s > 0
    has_down = s < S - 1
    fields = ((u_in, Ub), (v_in, Vb), (p_in, Pb))
    up_halo = [
        remote(a.at[pl.ds(0, RIM)], b.at[bottoms], halo_s.at[0, i], halo_r.at[0, i], (k, up))
        for i, (a, b) in enumerate(fields)
    ]
    down_halo = [
        remote(a.at[pl.ds(R - RIM, RIM)], b.at[tops], halo_s.at[1, i], halo_r.at[1, i], (k, down))
        for i, (a, b) in enumerate(fields)
    ]

    @pl.when(has_up)
    def _():
        for copy in up_halo:
            copy.start()

    @pl.when(has_down)
    def _():
        for copy in down_halo:
            copy.start()

    rate_copy = remote(rate_in.at[other], Rpar, rate_s, rate_r, (partner, s))
    rate_copy.start()
    before = lax.rem(k + n - 1, n)
    after = lax.rem(k + 1, n)
    shifts = [
        remote(u_in, Fn.at[0], shift_s.at[0], shift_r.at[0], (before, s)),
        remote(v_in, Fn.at[1], shift_s.at[1], shift_r.at[1], (before, s)),
    ]
    for copy in shifts:
        copy.start()

    zero = jnp.zeros((RIM, C), jnp.float32)
    Ub[0:RIM, :] = zero
    Ub[BASE + R + RIM : BASE + R + 2 * RIM, :] = zero
    W1[0:RIM, :] = zero
    W1[BASE + R + RIM : BASE + R + 2 * RIM, :] = zero

    @pl.when(jnp.logical_not(has_up))
    def _():
        Ub[BASE - RIM : BASE, :] = zero
        Vb[BASE - RIM : BASE, :] = zero
        Pb[BASE - RIM : BASE, :] = zero + 1.0
        Cb[0, BASE - RIM : BASE, :] = zero
        Cb[1, BASE - RIM : BASE, :] = zero

    @pl.when(jnp.logical_not(has_down))
    def _():
        Ub[BASE + R : BASE + R + RIM, :] = zero
        Vb[BASE + R : BASE + R + RIM, :] = zero
        Pb[BASE + R : BASE + R + RIM, :] = zero + 1.0
        Cb[0, BASE + R : BASE + R + RIM, :] = zero
        Cb[1, BASE + R : BASE + R + RIM, :] = zero

    loads[3].wait()
    rate_copy.wait_recv()
    for b in range(0, H, 8):
        own = jnp.exp(-Rown[b : b + 8, :] / n)
        par = jnp.exp(-Rpar[b : b + 8, :] / n)
        Rown[b : b + 8, :] = own
        Rpar[b : b + 8, :] = par
        Am[b : b + 8, :] = own * par

    def chunk(idx):
        return (
            pl.ds(pl.multiple_of((idx // cpr) * 8, 8), 8),
            pl.ds(pl.multiple_of((idx % cpr) * W, 128), W),
        )

    a_copies = []
    for d in range(1, nc):
        to = lax.rem(c + d, nc)
        rows, cols = chunk(to)
        copy = remote(Am.at[rows, cols], RA.at[d], a_s.at[d], a_r.at[d], (2 * to + j, s))
        copy.start()
        a_copies.append(copy)

    first = step0[0]
    cosines = [
        jnp.cos(
            jnp.float32(2.0 * jnp.pi / PERIOD)
            * jnp.full((8, 128), first + level, jnp.int32).astype(jnp.float32)
        )
        for level in range(STEPS)
    ]

    def depth_of(row):
        row = jnp.clip(row // TILE, 0, tile_rows - 1)
        return [mod[tmap[row, t]] for t in range(C // TILE)]

    def factors(depths):
        return [
            jnp.concatenate([1.0 + depth * cosines[level] for depth in depths], axis=1)
            for level in range(STEPS)
        ]

    first_row = s * R
    main_f = factors(depth_of(first_row))
    for copy in loads[:3]:
        copy.wait()

    def coefficients(base, fs):
        for level in range(STEPS):
            Q[level, base : base + 8, :] = time_step / (Pb[base : base + 8, :] * fs[level])

    for base in range(BASE, BASE + R, 8):
        coefficients(base, main_f)

    def first_step(base, keep):
        forcing = laplacian(Ub, base) - damping_rate * Vb[base : base + 8, :]
        speed = Vb[base : base + 8, :] + Q[0, base : base + 8, :] * forcing
        place = Ub[base : base + 8, :] + time_step * speed
        if keep is not None:
            place = place * keep
        Fo[0, base : base + 8, :] = forcing
        B1[base : base + 8, :] = speed
        U1[base : base + 8, :] = place

    for base in range(BASE + 8, BASE + R - 8, 8):
        first_step(base, None)

    @pl.when(has_down)
    def _():
        for copy in up_halo:
            copy.wait_recv()

    @pl.when(has_up)
    def _():
        for copy in down_halo:
            copy.wait_recv()

    coefficients(BASE - RIM, factors(depth_of(first_row - 1)))
    coefficients(BASE + R, factors(depth_of(first_row + R)))
    keep_top = has_up.astype(jnp.float32)
    keep_bottom = has_down.astype(jnp.float32)
    first_step(BASE - RIM, keep_top)
    first_step(BASE, None)
    first_step(BASE + R - 8, None)
    first_step(BASE + R, keep_bottom)

    for copy in shifts:
        copy.wait_recv()
    for base in range(BASE, BASE + R, 8):
        r = base - BASE
        forcing = laplacian(U1, base) - damping_rate * B1[base : base + 8, :]
        speed = B1[base : base + 8, :] + Q[1, base : base + 8, :] * forcing
        place = U1[base : base + 8, :] + time_step * speed
        Fo[1, base : base + 8, :] = forcing
        ends[0, r : r + 8, :] = place - Fn[0, r : r + 8, :]
        ends[1, r : r + 8, :] = speed - Fn[1, r : r + 8, :]

    m_copy = remote(ends.at[:, other], Mp, m_s, m_r, (partner, s))
    m_copy.start()
    m_copy.wait_recv()

    def half_rows(b):
        return pl.ds(pl.multiple_of(j * H + b, 8), 8)

    @pl.when(j == 0)
    def _():
        for b in range(0, H, 8):
            for f in range(2):
                E[f, b : b + 8, :] = (
                    ends[f, half_rows(b), :] + Rown[b : b + 8, :] * Mp[f, b : b + 8, :]
                )

    @pl.when(j == 1)
    def _():
        for b in range(0, H, 8):
            for f in range(2):
                E[f, b : b + 8, :] = (
                    Mp[f, b : b + 8, :] + Rpar[b : b + 8, :] * ends[f, half_rows(b), :]
                )

    e_copies = []
    for d in range(1, nc):
        to = lax.rem(c + d, nc)
        rows, cols = chunk(to)
        copy = remote(E.at[:, rows, cols], RE.at[d], e_s.at[d], e_r.at[d], (2 * to + j, s))
        copy.start()
        e_copies.append(copy)

    rows, cols = chunk(c)
    for copy in a_copies:
        copy.wait_recv()
    for copy in e_copies:
        copy.wait_recv()
    a0 = Am[rows, cols]
    total = a0
    state = [RE[1, f] for f in range(2)]
    total = total * RA[1]
    for d in range(2, nc):
        total = total * RA[d]
        state = [RA[d] * state[f] + RE[d, f] for f in range(2)]
    below = 1.0 / (1.0 - total)
    state = [(a0 * state[f] + E[f, rows, cols]) * below for f in range(2)]
    g_copies = []
    for d in range(1, nc):
        for f in range(2):
            X[d, f] = state[f]
        to = lax.rem(c - d + nc, nc)
        copy = remote(X.at[d], G.at[:, rows, cols], g_s.at[d], g_r.at[d], (2 * to + j, s))
        copy.start()
        g_copies.append(copy)
        state = [RA[d] * state[f] + RE[d, f] for f in range(2)]
    for f in range(2):
        G[f, rows, cols] = state[f]
    for copy in g_copies:
        copy.wait_recv()

    def main_half(b):
        return pl.ds(pl.multiple_of(BASE + j * H + b, 8), 8)

    @pl.when(j == 0)
    def _():
        for b in range(0, H, 8):
            for f in range(2):
                late = Rpar[b : b + 8, :] * G[f, b : b + 8, :] + Mp[f, b : b + 8, :]
                early = Rown[b : b + 8, :] * late + ends[f, half_rows(b), :]
                Cb[f, main_half(b), :] = early
                Cx[f, b : b + 8, :] = late

    @pl.when(j == 1)
    def _():
        for b in range(0, H, 8):
            for f in range(2):
                late = Rown[b : b + 8, :] * G[f, b : b + 8, :] + ends[f, half_rows(b), :]
                early = Rpar[b : b + 8, :] * late + Mp[f, b : b + 8, :]
                Cb[f, main_half(b), :] = late
                Cx[f, b : b + 8, :] = early

    main_mine = pl.ds(pl.multiple_of(BASE + j * H, 8), H)
    edge_cx = pl.ds(pl.multiple_of(j * (H - RIM), 8), RIM)
    edge_cb = pl.ds(pl.multiple_of(BASE + j * (R - RIM), 8), RIM)
    far = pl.ds(pl.multiple_of((1 - j) * (R + RIM) + BASE - RIM, 8), RIM)
    nb = lax.rem(s + 2 * j - 1 + S, S)
    c_copy = remote(Cx, Cb.at[:, main_mine], c_s, c_r, (partner, s))
    h_own = remote(Cb.at[:, edge_cb], Cb.at[:, far], h_s.at[0], h_r.at[j], (k, nb))
    h_par = remote(Cx.at[:, edge_cx], Cb.at[:, far], h_s.at[1], h_r.at[j], (partner, nb))
    sends_halo = jnp.where(j == 0, has_up.astype(jnp.int32), has_down.astype(jnp.int32)) == 1

    @pl.when(sends_halo)
    def _():
        h_own.start()
        h_par.start()

    c_copy.start()
    c_copy.wait_recv()
    p_copy = remote(Cb.at[:, pl.ds(BASE, R)], Pre, p_s, p_r, (after, s))
    p_copy.start()

    acc = jnp.zeros((8, C), jnp.float32)
    cos_cols = [jnp.concatenate([cosine] * (C // TILE), axis=1) for cosine in cosines]

    def weigh(base):
        total_v = Cb[1, base : base + 8, :] + time_step * Cb[0, base : base + 8, :]
        q = Q[1, base : base + 8, :]
        W1[base : base + 8, :] = q * total_v
        B1[base : base + 8, :] = (1.0 - damping_rate * q) * total_v
        return total_v, q

    for base in range(BASE, BASE + R, 8):
        total_v, q = weigh(base)
        acc = acc + Pb[base : base + 8, :] * cos_cols[1] * total_v * Fo[1, base : base + 8, :] * (q * q)

    @pl.when(has_up)
    def _():
        remote(Cb.at[:, edge_cb], Cb.at[:, tops], h_s.at[0], h_r.at[1], (k, nb)).wait_recv()

    @pl.when(has_down)
    def _():
        remote(Cb.at[:, edge_cb], Cb.at[:, bottoms], h_s.at[0], h_r.at[0], (k, nb)).wait_recv()

    weigh(BASE - RIM)
    weigh(BASE + R)

    def second(base, keep):
        back_u = Cb[0, base : base + 8, :] + laplacian(W1, base)
        total_v = B1[base : base + 8, :] + time_step * back_u
        q = Q[0, base : base + 8, :]
        weighted = q * total_v
        if keep is not None:
            weighted = weighted * keep
        W0[base : base + 8, :] = weighted
        return back_u, total_v, q

    second(BASE - RIM, keep_top)
    second(BASE + R, keep_bottom)
    for base in range(BASE, BASE + R, 8):
        r = base - BASE
        back_u, total_v, q = second(base, None)
        U1[base : base + 8, :] = back_u
        B1[base : base + 8, :] = (1.0 - damping_rate * q) * total_v
        acc = acc + Pb[base : base + 8, :] * cos_cols[0] * total_v * Fo[0, base : base + 8, :] * (q * q)

    lane = lax.broadcasted_iota(jnp.int32, (8, 128), 1)
    tile_row = first_row // TILE
    share = jnp.zeros((8, 128), jnp.float32)
    for t in range(C // TILE):
        summed = jnp.sum(acc[:, t * TILE : (t + 1) * TILE], axis=1, keepdims=True)
        share = share + jnp.where(lane == tmap[tile_row, t], summed, 0.0)
    part[0] = share * (-1.0 / time_step)
    d1 = []
    for d in range(1, nc):
        copy = remote(part.at[0], gat1.at[d], d1_s.at[d], d1_r.at[d], (chip(d), s))
        copy.start()
        d1.append(copy)

    p_copy.wait_recv()
    for base in range(BASE, BASE + R, 8):
        r = base - BASE
        out_u[r : r + 8, :] = U1[base : base + 8, :] + laplacian(W0, base) - Pre[0, r : r + 8, :]
        out_v[r : r + 8, :] = B1[base : base + 8, :] - Pre[1, r : r + 8, :]

    for copy in d1:
        copy.wait_recv()
    share = part[0]
    for d in range(1, nc):
        share = share + gat1[d]
    part[1] = share
    d2 = []
    for d in range(1, 2 * S):
        at = lax.rem(s * 2 + j + d, 2 * S)
        copy = remote(part.at[1], gat2.at[d], d2_s.at[d], d2_r.at[d], (2 * c + at % 2, at // 2))
        copy.start()
        d2.append(copy)
    for copy in d2:
        copy.wait_recv()
    for d in range(1, 2 * S):
        share = share + gat2[d]
    out_g[...] = jnp.sum(share, axis=0, keepdims=True)

    @pl.when(has_up)
    def _():
        for copy in up_halo:
            copy.wait_send()

    @pl.when(has_down)
    def _():
        for copy in down_halo:
            copy.wait_send()

    @pl.when(sends_halo)
    def _():
        h_own.wait_send()
        h_par.wait_send()

    for copy in [rate_copy, *shifts, *a_copies, m_copy, *e_copies, *g_copies, c_copy, p_copy, *d1, *d2]:
        copy.wait_send()


def solution(mesh):
    n = mesh.shape["tm"]
    S = mesh.shape["strip"]
    nc = n // 2

    def shards(forward_u, forward_v, permittivity, coarse_rate, modulation, tile_map, start_step):
        R, C = permittivity.shape
        H = R // 2
        W = H * C // (8 * nc)
        assert TILE % R == 0 and W % 128 == 0 and C % W == 0
        f32 = jnp.float32
        ext = R + 2 * BASE
        vmem = lambda *shape: pltpu.VMEM(shape, f32)
        dma = lambda *shape: pltpu.SemaphoreType.DMA(shape)
        any_spec = pl.BlockSpec(memory_space=pl.ANY)
        smem = pl.BlockSpec(memory_space=pltpu.SMEM)
        whole = pl.BlockSpec(memory_space=pltpu.VMEM)
        out_u, out_v, out_g = pl.pallas_call(
            functools.partial(kernel, n, S, tile_map.shape[0]),
            out_shape=(
                jax.ShapeDtypeStruct((R, C), f32),
                jax.ShapeDtypeStruct((R, C), f32),
                jax.ShapeDtypeStruct((1, 128), f32),
            ),
            in_specs=[any_spec] * 4 + [smem] * 3,
            out_specs=(whole, whole, whole),
            scratch_shapes=[
                vmem(ext, C), vmem(ext, C), vmem(ext, C), vmem(2, ext, C), vmem(2, ext, C),
                vmem(ext, C), vmem(2, ext, C), vmem(ext, C), vmem(ext, C), vmem(ext, C),
                vmem(2, R, C), vmem(2, R, C), vmem(H, C), vmem(H, C), vmem(H, C),
                vmem(2, H, C), vmem(2, H, C), vmem(nc, 8, W), vmem(nc, 2, 8, W),
                vmem(nc, 2, 8, W), vmem(2, H, C), vmem(2, H, C), vmem(2, R, C),
                vmem(2, 8, 128), vmem(nc, 8, 128), vmem(2 * S, 8, 128),
                dma(4), dma(2, 3), dma(2, 3), dma(2), dma(2), dma(), dma(), dma(nc), dma(nc),
                dma(), dma(), dma(nc), dma(nc), dma(nc), dma(nc), dma(), dma(), dma(2), dma(2),
                dma(), dma(), dma(nc), dma(nc), dma(2 * S), dma(2 * S),
            ],
            compiler_params=pltpu.CompilerParams(
                collective_id=0, has_side_effects=True, vmem_limit_bytes=48 * 1024 * 1024
            ),
        )(forward_u[0], forward_v[0], permittivity, coarse_rate[0], modulation, tile_map, start_step)
        return out_u[None], out_v[None], out_g[0, : modulation.shape[0]]

    placed = (
        P("tm", "strip", None),
        P("tm", "strip", None),
        P("strip", None),
        P("tm", "strip", None),
        P(),
        P(),
        P("tm"),
    )
    return jax.shard_map(
        shards,
        mesh=mesh,
        in_specs=placed,
        out_specs=(P("tm", "strip", None), P("tm", "strip", None), P()),
        check_vma=False,
    )
```

```python
import functools

import jax
import jax.numpy as jnp
from jax import lax
from jax.experimental import pallas as pl
from jax.experimental.pallas import tpu as pltpu
from jax.sharding import PartitionSpec as P

TILE = 128
STEPS = 2
STENCIL = 4
PERIOD = 256
RIM = STEPS * STENCIL
BASE = 2 * RIM

stencil_coef = (-205.0 / 72.0, 8.0 / 5.0, -1.0 / 5.0, 8.0 / 315.0, -1.0 / 560.0)
time_step = 0.4
damping_rate = 0.1

MESH = pl.DeviceIdType.MESH


def laplacian(ref, base):
    center = ref[base : base + 8, :]
    cols = center.shape[1]
    summed = (2.0 * stencil_coef[0]) * center
    for o in range(1, STENCIL + 1):
        along_x = ref[base + o : base + o + 8, :] + ref[base - o : base - o + 8, :]
        along_y = pltpu.roll(center, o, 1) + pltpu.roll(center, cols - o, 1)
        summed = summed + stencil_coef[o] * (along_x + along_y)
    return summed


def kernel(
    n, S, tile_rows,
    u_in, v_in, p_in, rate_in, mod_in, tmap_in, step_in,
    out_u, out_v, out_g,
    Ub, Vb, Pb, Q, Fo, U1, Cb, W1, B1, W0, Fp, ends, R0, R1, Am, Mp, Ep, E, RA, RE, X, G, Cx, Pre,
    part, gat1, gat2, mod, tmap, step0,
    load_sem, halo_s, halo_r, shift_s, shift_r, rate_s, rate_r, a_s, a_r, m_s, m_r, e_s, e_r,
    g_s, g_r, c_s, c_r, h_s, h_r, p_s, p_r, d1_s, d1_r, d2_s, d2_r,
):
    k = lax.axis_index("tm")
    s = lax.axis_index("strip")
    nc = n // 2
    c = k // 2
    j = k % 2
    partner = 2 * c + 1 - j
    R, C = out_u.shape
    H = R // 2
    W = H * C // (8 * nc)
    cpr = C // W

    def chip(d):
        return 2 * lax.rem(c + d + nc, nc) + j

    mine = pl.ds(pl.multiple_of(j * H, 8), H)
    other = pl.ds(pl.multiple_of((1 - j) * H, 8), H)
    loads = [
        pltpu.make_async_copy(u_in, Ub.at[pl.ds(BASE, R)], load_sem.at[0]),
        pltpu.make_async_copy(v_in, Vb.at[pl.ds(BASE, R)], load_sem.at[1]),
        pltpu.make_async_copy(p_in, Pb.at[pl.ds(BASE, R)], load_sem.at[2]),
        pltpu.make_async_copy(mod_in, mod, load_sem.at[4]),
        pltpu.make_async_copy(tmap_in, tmap, load_sem.at[5]),
        pltpu.make_async_copy(step_in, step0, load_sem.at[6]),
    ]
    for load in loads:
        load.start()

    own_rate = pltpu.make_async_copy(rate_in.at[pl.ds(0, H)], R0, load_sem.at[3])

    @pl.when(j == 0)
    def _():
        own_rate.start()

    barrier = pltpu.get_barrier_semaphore()
    for d in range(1, nc):
        pl.semaphore_signal(barrier, inc=1, device_id=(chip(d), s), device_id_type=MESH)
    for d in range(1, 2 * S):
        at = lax.rem(s * 2 + j + d, 2 * S)
        pl.semaphore_signal(
            barrier, inc=1, device_id=(2 * c + at % 2, at // 2), device_id_type=MESH
        )
    aside = lax.rem(k + 2 * j - 1 + n, n)
    pl.semaphore_signal(barrier, inc=1, device_id=(aside, s), device_id_type=MESH)
    pl.semaphore_wait(barrier, (nc - 1) + (2 * S - 1) + 1)

    def remote(src, dst, ss, rs, where):
        return pltpu.make_async_remote_copy(
            src_ref=src, dst_ref=dst, send_sem=ss, recv_sem=rs,
            device_id=where, device_id_type=MESH,
        )

    up = lax.rem(s + S - 1, S)
    down = lax.rem(s + 1, S)
    tops = pl.ds(BASE - RIM, RIM)
    bottoms = pl.ds(BASE + R, RIM)
    has_up = s > 0
    has_down = s < S - 1
    fields = ((u_in, Ub), (v_in, Vb), (p_in, Pb))
    up_halo = [
        remote(a.at[pl.ds(0, RIM)], b.at[bottoms], halo_s.at[0, i], halo_r.at[0, i], (k, up))
        for i, (a, b) in enumerate(fields)
    ]
    down_halo = [
        remote(a.at[pl.ds(R - RIM, RIM)], b.at[tops], halo_s.at[1, i], halo_r.at[1, i], (k, down))
        for i, (a, b) in enumerate(fields)
    ]

    @pl.when(has_up)
    def _():
        for copy in up_halo:
            copy.start()

    @pl.when(has_down)
    def _():
        for copy in down_halo:
            copy.start()

    low = pl.ds(0, H)
    high = pl.ds(H, H)
    c_next = lax.rem(c + 1, nc)
    rate_pair = remote(rate_in.at[high], R0, rate_s.at[0], rate_r.at[0], (partner, s))
    rate_next = [
        remote(rate_in.at[low], R1, rate_s.at[0], rate_r.at[1], (2 * c_next, s)),
        remote(rate_in.at[high], R1, rate_s.at[1], rate_r.at[1], (2 * c_next + 1, s)),
    ]

    @pl.when(j == 0)
    def _():
        rate_pair.start()

    @pl.when(j == 1)
    def _():
        for copy in rate_next:
            copy.start()

    shifts = [
        remote(u_in.at[other], Fp.at[0], shift_s.at[0], shift_r.at[0], (partner, s)),
        remote(v_in.at[other], Fp.at[1], shift_s.at[1], shift_r.at[1], (partner, s)),
    ]
    for copy in shifts:
        copy.start()

    zero = jnp.zeros((RIM, C), jnp.float32)
    Ub[0:RIM, :] = zero
    Ub[BASE + R + RIM : BASE + R + 2 * RIM, :] = zero
    W1[0:RIM, :] = zero
    W1[BASE + R + RIM : BASE + R + 2 * RIM, :] = zero

    @pl.when(jnp.logical_not(has_up))
    def _():
        Ub[BASE - RIM : BASE, :] = zero
        Vb[BASE - RIM : BASE, :] = zero
        Pb[BASE - RIM : BASE, :] = zero + 1.0
        Cb[0, BASE - RIM : BASE, :] = zero
        Cb[1, BASE - RIM : BASE, :] = zero

    @pl.when(jnp.logical_not(has_down))
    def _():
        Ub[BASE + R : BASE + R + RIM, :] = zero
        Vb[BASE + R : BASE + R + RIM, :] = zero
        Pb[BASE + R : BASE + R + RIM, :] = zero + 1.0
        Cb[0, BASE + R : BASE + R + RIM, :] = zero
        Cb[1, BASE + R : BASE + R + RIM, :] = zero

    def chunk(idx):
        return (
            pl.ds(pl.multiple_of((idx // cpr) * 8, 8), 8),
            pl.ds(pl.multiple_of((idx % cpr) * W, 128), W),
        )

    for copy in loads[3:]:
        copy.wait()
    first = step0[0]
    cosines = [
        jnp.cos(
            jnp.float32(2.0 * jnp.pi / PERIOD)
            * jnp.full((8, 128), first + level, jnp.int32).astype(jnp.float32)
        )
        for level in range(STEPS)
    ]

    def depth_of(row):
        row = jnp.clip(row // TILE, 0, tile_rows - 1)
        return [mod[tmap[row, t]] for t in range(C // TILE)]

    def factors(depths):
        return [
            jnp.concatenate([1.0 + depth * cosines[level] for depth in depths], axis=1)
            for level in range(STEPS)
        ]

    first_row = s * R
    main_f = factors(depth_of(first_row))
    for copy in loads[:3]:
        copy.wait()

    def coefficients(base, fs):
        for level in range(STEPS):
            Q[level, base : base + 8, :] = time_step / (Pb[base : base + 8, :] * fs[level])

    for base in range(BASE, BASE + R, 8):
        coefficients(base, main_f)

    def first_step(base, keep):
        forcing = laplacian(Ub, base) - damping_rate * Vb[base : base + 8, :]
        speed = Vb[base : base + 8, :] + Q[0, base : base + 8, :] * forcing
        place = Ub[base : base + 8, :] + time_step * speed
        if keep is not None:
            place = place * keep
        Fo[0, base : base + 8, :] = forcing
        B1[base : base + 8, :] = speed
        U1[base : base + 8, :] = place

    for base in range(BASE + 8, BASE + R - 8, 8):
        first_step(base, None)

    @pl.when(j == 0)
    def _():
        own_rate.wait()

    @pl.when(j == 1)
    def _():
        rate_pair.wait_recv()

    rate_next[0].wait_recv()
    for b in range(0, H, 8):
        own = jnp.exp(-R0[b : b + 8, :] / n)
        R0[b : b + 8, :] = own
        entering = jnp.exp(-R1[b : b + 8, :] / n)
        R1[b : b + 8, :] = entering
        Am[b : b + 8, :] = own * entering
    a_copies = []
    for d in range(1, nc):
        to = lax.rem(c + d, nc)
        rows, cols = chunk(to)
        copy = remote(Am.at[rows, cols], RA.at[d], a_s.at[d], a_r.at[d], (2 * to + j, s))
        copy.start()
        a_copies.append(copy)

    @pl.when(has_down)
    def _():
        for copy in up_halo:
            copy.wait_recv()

    @pl.when(has_up)
    def _():
        for copy in down_halo:
            copy.wait_recv()

    coefficients(BASE - RIM, factors(depth_of(first_row - 1)))
    coefficients(BASE + R, factors(depth_of(first_row + R)))
    keep_top = has_up.astype(jnp.float32)
    keep_bottom = has_down.astype(jnp.float32)
    first_step(BASE - RIM, keep_top)
    first_step(BASE, None)
    first_step(BASE + R - 8, None)
    first_step(BASE + R, keep_bottom)

    for base in range(BASE, BASE + R, 8):
        r = base - BASE
        forcing = laplacian(U1, base) - damping_rate * B1[base : base + 8, :]
        speed = B1[base : base + 8, :] + Q[1, base : base + 8, :] * forcing
        place = U1[base : base + 8, :] + time_step * speed
        Fo[1, base : base + 8, :] = forcing
        ends[0, r : r + 8, :] = place
        ends[1, r : r + 8, :] = speed

    m_copy = remote(ends.at[:, other], Mp, m_s, m_r, (partner, s))
    m_copy.start()
    for copy in shifts:
        copy.wait_recv()
    m_copy.wait_recv()

    def main_half(b):
        return pl.ds(pl.multiple_of(BASE + j * H + b, 8), 8)

    starts = (Ub, Vb)

    @pl.when(j == 0)
    def _():
        for b in range(0, H, 8):
            entering = R1[b : b + 8, :]
            for f in range(2):
                term = (
                    ends[f, b : b + 8, :] - Fp[f, b : b + 8, :] + R0[b : b + 8, :] * Mp[f, b : b + 8, :]
                )
                Ep[f, b : b + 8, :] = term
                E[f, b : b + 8, :] = entering * term - starts[f][BASE + b : BASE + b + 8, :]

    @pl.when(j == 1)
    def _():
        for b in range(0, H, 8):
            entering = R1[b : b + 8, :]
            for f in range(2):
                term = (
                    Mp[f, b : b + 8, :]
                    - starts[f][BASE + H + b : BASE + H + b + 8, :]
                    + R0[b : b + 8, :] * ends[f, H + b : H + b + 8, :]
                )
                Ep[f, b : b + 8, :] = term
                E[f, b : b + 8, :] = entering * term - Fp[f, b : b + 8, :]

    e_copies = []
    for d in range(1, nc):
        to = lax.rem(c + d, nc)
        rows, cols = chunk(to)
        copy = remote(E.at[:, rows, cols], RE.at[d], e_s.at[d], e_r.at[d], (2 * to + j, s))
        copy.start()
        e_copies.append(copy)

    rows, cols = chunk(c)
    for copy in a_copies:
        copy.wait_recv()
    for copy in e_copies:
        copy.wait_recv()
    a0 = Am[rows, cols]
    total = a0
    state = [RE[1, f] for f in range(2)]
    total = total * RA[1]
    for d in range(2, nc):
        total = total * RA[d]
        state = [RA[d] * state[f] + RE[d, f] for f in range(2)]
    below = 1.0 / (1.0 - total)
    state = [(a0 * state[f] + E[f, rows, cols]) * below for f in range(2)]
    g_copies = []
    for d in range(1, nc):
        for f in range(2):
            X[d, f] = state[f]
        to = lax.rem(c - d + nc, nc)
        copy = remote(X.at[d], G.at[:, rows, cols], g_s.at[d], g_r.at[d], (2 * to + j, s))
        copy.start()
        g_copies.append(copy)
        state = [RA[d] * state[f] + RE[d, f] for f in range(2)]
    for f in range(2):
        G[f, rows, cols] = state[f]
    for copy in g_copies:
        copy.wait_recv()

    @pl.when(j == 0)
    def _():
        for b in range(0, H, 8):
            for f in range(2):
                value = G[f, b : b + 8, :]
                Cx[f, b : b + 8, :] = value + Mp[f, b : b + 8, :]
                Cb[f, BASE + b : BASE + b + 8, :] = R0[b : b + 8, :] * value + Ep[f, b : b + 8, :]

    @pl.when(j == 1)
    def _():
        for b in range(0, H, 8):
            for f in range(2):
                value = G[f, b : b + 8, :]
                early = R0[b : b + 8, :] * value + Ep[f, b : b + 8, :]
                Cb[f, BASE + H + b : BASE + H + b + 8, :] = value + ends[f, H + b : H + b + 8, :]
                Cx[f, b : b + 8, :] = early
                Pre[f, H + b : H + b + 8, :] = early

    main_mine = pl.ds(pl.multiple_of(BASE + j * H, 8), H)
    edge_cx = pl.ds(pl.multiple_of(j * (H - RIM), 8), RIM)
    edge_cb = pl.ds(pl.multiple_of(BASE + j * (R - RIM), 8), RIM)
    far = pl.ds(pl.multiple_of((1 - j) * (R + RIM) + BASE - RIM, 8), RIM)
    nb = lax.rem(s + 2 * j - 1 + S, S)
    c_copy = remote(Cx, Cb.at[:, main_mine], c_s, c_r, (partner, s))
    h_own = remote(Cb.at[:, edge_cb], Cb.at[:, far], h_s.at[0], h_r.at[j], (k, nb))
    h_par = remote(Cx.at[:, edge_cx], Cb.at[:, far], h_s.at[1], h_r.at[j], (partner, nb))
    sends_halo = jnp.where(j == 0, has_up.astype(jnp.int32), has_down.astype(jnp.int32)) == 1

    @pl.when(sends_halo)
    def _():
        h_own.start()
        h_par.start()

    c_copy.start()
    p_low = remote(Cx, Pre.at[:, low], p_s.at[0], p_r.at[0], (2 * c_next, s))
    p_pair = remote(Cb.at[:, main_mine], Pre.at[:, low], p_s.at[1], p_r.at[0], (partner, s))
    p_high = remote(Cb.at[:, main_mine], Pre.at[:, high], p_s.at[0], p_r.at[1], (2 * c_next, s))

    @pl.when(j == 0)
    def _():
        p_low.start()
        p_pair.start()

    @pl.when(j == 1)
    def _():
        p_high.start()

    c_copy.wait_recv()

    acc = jnp.zeros((8, C), jnp.float32)
    cos_cols = [jnp.concatenate([cosine] * (C // TILE), axis=1) for cosine in cosines]

    def weigh(base):
        total_v = Cb[1, base : base + 8, :] + time_step * Cb[0, base : base + 8, :]
        q = Q[1, base : base + 8, :]
        W1[base : base + 8, :] = q * total_v
        B1[base : base + 8, :] = (1.0 - damping_rate * q) * total_v
        return total_v, q

    for base in range(BASE, BASE + R, 8):
        total_v, q = weigh(base)
        acc = acc + Pb[base : base + 8, :] * cos_cols[1] * total_v * Fo[1, base : base + 8, :] * (q * q)

    def second(base, keep):
        back_u = Cb[0, base : base + 8, :] + laplacian(W1, base)
        total_v = B1[base : base + 8, :] + time_step * back_u
        q = Q[0, base : base + 8, :]
        weighted = q * total_v
        if keep is not None:
            weighted = weighted * keep
        W0[base : base + 8, :] = weighted
        return back_u, total_v, q

    def inner(base):
        back_u, total_v, q = second(base, None)
        U1[base : base + 8, :] = back_u
        B1[base : base + 8, :] = (1.0 - damping_rate * q) * total_v
        return Pb[base : base + 8, :] * cos_cols[0] * total_v * Fo[0, base : base + 8, :] * (q * q)

    for base in range(BASE + 8, BASE + R - 8, 8):
        acc = acc + inner(base)

    @pl.when(has_up)
    def _():
        remote(Cb.at[:, edge_cb], Cb.at[:, tops], h_s.at[0], h_r.at[1], (k, nb)).wait_recv()

    @pl.when(has_down)
    def _():
        remote(Cb.at[:, edge_cb], Cb.at[:, bottoms], h_s.at[0], h_r.at[0], (k, nb)).wait_recv()

    weigh(BASE - RIM)
    weigh(BASE + R)
    second(BASE - RIM, keep_top)
    second(BASE + R, keep_bottom)
    acc = acc + inner(BASE)
    acc = acc + inner(BASE + R - 8)

    lane = lax.broadcasted_iota(jnp.int32, (8, 128), 1)
    tile_row = first_row // TILE
    share = jnp.zeros((8, 128), jnp.float32)
    for t in range(C // TILE):
        summed = jnp.sum(acc[:, t * TILE : (t + 1) * TILE], axis=1, keepdims=True)
        share = share + jnp.where(lane == tmap[tile_row, t], summed, 0.0)
    part[0] = share * (-1.0 / time_step)
    d1 = []
    for d in range(1, nc):
        copy = remote(part.at[0], gat1.at[d], d1_s.at[d], d1_r.at[d], (chip(d), s))
        copy.start()
        d1.append(copy)

    for base in range(BASE, BASE + R, 8):
        U1[base : base + 8, :] = U1[base : base + 8, :] + laplacian(W0, base)

    for copy in d1:
        copy.wait_recv()
    share = part[0]
    for d in range(1, nc):
        share = share + gat1[d]
    part[1] = share
    d2 = []
    for d in range(1, 2 * S):
        at = lax.rem(s * 2 + j + d, 2 * S)
        copy = remote(part.at[1], gat2.at[d], d2_s.at[d], d2_r.at[d], (2 * c + at % 2, at // 2))
        copy.start()
        d2.append(copy)
    p_low.wait_recv()

    @pl.when(j == 0)
    def _():
        p_high.wait_recv()

    for base in range(BASE, BASE + R, 8):
        r = base - BASE
        out_u[r : r + 8, :] = U1[base : base + 8, :] - Pre[0, r : r + 8, :]
        out_v[r : r + 8, :] = B1[base : base + 8, :] - Pre[1, r : r + 8, :]
    for copy in d2:
        copy.wait_recv()
    for d in range(1, 2 * S):
        share = share + gat2[d]
    out_g[...] = jnp.sum(share, axis=0, keepdims=True)

    @pl.when(has_up)
    def _():
        for copy in up_halo:
            copy.wait_send()

    @pl.when(has_down)
    def _():
        for copy in down_halo:
            copy.wait_send()

    @pl.when(sends_halo)
    def _():
        h_own.wait_send()
        h_par.wait_send()

    @pl.when(j == 0)
    def _():
        rate_pair.wait_send()
        p_low.wait_send()
        p_pair.wait_send()

    @pl.when(j == 1)
    def _():
        for copy in [*rate_next, p_high]:
            copy.wait_send()

    for copy in [*shifts, *a_copies, m_copy, *e_copies, *g_copies, c_copy, *d1, *d2]:
        copy.wait_send()


def store_outputs(u, v, g, out_u, out_v, out_g, sems):
    pairs = ((u, out_u), (v, out_v), (g, out_g))
    copies = [pltpu.make_async_copy(a, b, sems.at[i]) for i, (a, b) in enumerate(pairs)]
    for copy in copies:
        copy.start()
    for copy in copies:
        copy.wait()


def solution(mesh):
    n = mesh.shape["tm"]
    S = mesh.shape["strip"]
    nc = n // 2

    def shards(forward_u, forward_v, permittivity, coarse_rate, modulation, tile_map, start_step):
        R, C = permittivity.shape
        H = R // 2
        W = H * C // (8 * nc)
        assert TILE % R == 0 and W % 128 == 0 and C % W == 0
        f32 = jnp.float32
        ext = R + 2 * BASE
        vmem = lambda *shape: pltpu.VMEM(shape, f32)
        dma = lambda *shape: pltpu.SemaphoreType.DMA(shape)
        any_spec = pl.BlockSpec(memory_space=pl.ANY)
        hbm = pl.BlockSpec(memory_space=pltpu.HBM)
        whole = pl.BlockSpec(memory_space=pltpu.VMEM)
        out_u, out_v, out_g = pl.pallas_call(
            functools.partial(kernel, n, S, tile_map.shape[0]),
            out_shape=(
                jax.ShapeDtypeStruct((R, C), f32),
                jax.ShapeDtypeStruct((R, C), f32),
                jax.ShapeDtypeStruct((1, 128), f32),
            ),
            in_specs=[hbm] * 7,
            out_specs=(whole, whole, whole),
            scratch_shapes=[
                vmem(ext, C), vmem(ext, C), vmem(ext, C), vmem(2, ext, C), vmem(2, ext, C),
                vmem(ext, C), vmem(2, ext, C), vmem(ext, C), vmem(ext, C), vmem(ext, C),
                vmem(2, H, C), vmem(2, R, C), vmem(H, C), vmem(H, C), vmem(H, C),
                vmem(2, H, C), vmem(2, H, C), vmem(2, H, C), vmem(nc, 8, W), vmem(nc, 2, 8, W),
                vmem(nc, 2, 8, W), vmem(2, H, C), vmem(2, H, C), vmem(2, R, C),
                vmem(2, 8, 128), vmem(nc, 8, 128), vmem(2 * S, 8, 128),
                pltpu.SMEM(modulation.shape, f32), pltpu.SMEM(tile_map.shape, jnp.int32),
                pltpu.SMEM(start_step.shape, jnp.int32),
                dma(7), dma(2, 3), dma(2, 3), dma(2), dma(2), dma(2), dma(2), dma(nc), dma(nc),
                dma(), dma(), dma(nc), dma(nc), dma(nc), dma(nc), dma(), dma(), dma(2), dma(2),
                dma(2), dma(2), dma(nc), dma(nc), dma(2 * S), dma(2 * S),
            ],
            compiler_params=pltpu.CompilerParams(
                collective_id=0, has_side_effects=True, vmem_limit_bytes=48 * 1024 * 1024
            ),
        )(forward_u[0], forward_v[0], permittivity, coarse_rate[0], modulation, tile_map, start_step)
        out_u, out_v, out_g = pl.pallas_call(
            store_outputs,
            out_shape=(
                jax.ShapeDtypeStruct((R, C), f32),
                jax.ShapeDtypeStruct((R, C), f32),
                jax.ShapeDtypeStruct((1, 128), f32),
            ),
            in_specs=[any_spec] * 3,
            out_specs=(any_spec,) * 3,
            scratch_shapes=[dma(3)],
        )(out_u, out_v, out_g)
        return out_u[None], out_v[None], out_g[0, : modulation.shape[0]]

    placed = (
        P("tm", "strip", None),
        P("tm", "strip", None),
        P("strip", None),
        P("tm", "strip", None),
        P(),
        P(),
        P("tm"),
    )
    return jax.shard_map(
        shards,
        mesh=mesh,
        in_specs=placed,
        out_specs=(P("tm", "strip", None), P("tm", "strip", None), P()),
        check_vma=False,
    )
```

```python
import functools

import jax
import jax.numpy as jnp
from jax import lax
from jax.experimental import pallas as pl
from jax.experimental.pallas import tpu as pltpu
from jax.sharding import PartitionSpec as P

TILE = 128
STEPS = 2
STENCIL = 4
PERIOD = 256
RIM = STEPS * STENCIL
BASE = 2 * RIM

stencil_coef = (-205.0 / 72.0, 8.0 / 5.0, -1.0 / 5.0, 8.0 / 315.0, -1.0 / 560.0)
time_step = 0.4
damping_rate = 0.1

MESH = pl.DeviceIdType.MESH


def laplacian(ref, base):
    center = ref[base : base + 8, :]
    cols = center.shape[1]
    summed = (2.0 * stencil_coef[0]) * center
    for o in range(1, STENCIL + 1):
        along_x = ref[base + o : base + o + 8, :] + ref[base - o : base - o + 8, :]
        along_y = pltpu.roll(center, o, 1) + pltpu.roll(center, cols - o, 1)
        summed = summed + stencil_coef[o] * (along_x + along_y)
    return summed


def kernel(
    n, S, tile_rows,
    u_in, v_in, p_in, rate_in, mod_in, tmap_in, step_in,
    out_u, out_v, out_g,
    Ub, Vb, Pb, Q, Fo, U1, Cb, W1, B1, W0, Fp, ends, R0, R1, Am, Mp, Ep, E, RA, RE, X, G, Cx, Pre,
    part, gat1, gat2, mod, tmap, step0,
    load_sem, halo_s, halo_r, shift_s, shift_r, rate_s, rate_r, a_s, a_r, m_s, m_r, e_s, e_r,
    g_s, g_r, c_s, c_r, h_s, h_r, p_s, p_r, d1_s, d1_r, d2_s, d2_r,
):
    k = lax.axis_index("tm")
    s = lax.axis_index("strip")
    nc = n // 2
    c = k // 2
    j = k % 2
    partner = 2 * c + 1 - j
    R, C = out_u.shape
    H = R // 2
    W = H * C // (8 * nc)
    cpr = C // W

    def chip(d):
        return 2 * lax.rem(c + d + nc, nc) + j

    mine = pl.ds(pl.multiple_of(j * H, 8), H)
    other = pl.ds(pl.multiple_of((1 - j) * H, 8), H)
    loads = [
        pltpu.make_async_copy(u_in, Ub.at[pl.ds(BASE, R)], load_sem.at[0]),
        pltpu.make_async_copy(v_in, Vb.at[pl.ds(BASE, R)], load_sem.at[1]),
        pltpu.make_async_copy(p_in, Pb.at[pl.ds(BASE, R)], load_sem.at[2]),
        pltpu.make_async_copy(mod_in, mod, load_sem.at[4]),
        pltpu.make_async_copy(tmap_in, tmap, load_sem.at[5]),
        pltpu.make_async_copy(step_in, step0, load_sem.at[6]),
    ]
    for load in loads:
        load.start()

    own_rate = pltpu.make_async_copy(rate_in.at[pl.ds(0, H)], R0, load_sem.at[3])

    @pl.when(j == 0)
    def _():
        own_rate.start()

    barrier = pltpu.get_barrier_semaphore()
    for d in range(1, nc):
        pl.semaphore_signal(barrier, inc=1, device_id=(chip(d), s), device_id_type=MESH)
    for d in range(1, 2 * S):
        at = lax.rem(s * 2 + j + d, 2 * S)
        pl.semaphore_signal(
            barrier, inc=1, device_id=(2 * c + at % 2, at // 2), device_id_type=MESH
        )
    aside = lax.rem(k + 2 * j - 1 + n, n)
    pl.semaphore_signal(barrier, inc=1, device_id=(aside, s), device_id_type=MESH)
    pl.semaphore_wait(barrier, (nc - 1) + (2 * S - 1) + 1)

    def remote(src, dst, ss, rs, where):
        return pltpu.make_async_remote_copy(
            src_ref=src, dst_ref=dst, send_sem=ss, recv_sem=rs,
            device_id=where, device_id_type=MESH,
        )

    up = lax.rem(s + S - 1, S)
    down = lax.rem(s + 1, S)
    tops = pl.ds(BASE - RIM, RIM)
    bottoms = pl.ds(BASE + R, RIM)
    has_up = s > 0
    has_down = s < S - 1
    fields = ((u_in, Ub), (v_in, Vb), (p_in, Pb))
    up_halo = [
        remote(a.at[pl.ds(0, RIM)], b.at[bottoms], halo_s.at[0, i], halo_r.at[0, i], (k, up))
        for i, (a, b) in enumerate(fields)
    ]
    down_halo = [
        remote(a.at[pl.ds(R - RIM, RIM)], b.at[tops], halo_s.at[1, i], halo_r.at[1, i], (k, down))
        for i, (a, b) in enumerate(fields)
    ]

    @pl.when(has_up)
    def _():
        for copy in up_halo:
            copy.start()

    @pl.when(has_down)
    def _():
        for copy in down_halo:
            copy.start()

    low = pl.ds(0, H)
    high = pl.ds(H, H)
    c_next = lax.rem(c + 1, nc)
    rate_pair = remote(rate_in.at[high], R0, rate_s.at[0], rate_r.at[0], (partner, s))
    rate_next = [
        remote(rate_in.at[low], R1, rate_s.at[0], rate_r.at[1], (2 * c_next, s)),
        remote(rate_in.at[high], R1, rate_s.at[1], rate_r.at[1], (2 * c_next + 1, s)),
    ]

    @pl.when(j == 0)
    def _():
        rate_pair.start()

    @pl.when(j == 1)
    def _():
        for copy in rate_next:
            copy.start()

    shifts = [
        remote(u_in.at[other], Fp.at[0], shift_s.at[0], shift_r.at[0], (partner, s)),
        remote(v_in.at[other], Fp.at[1], shift_s.at[1], shift_r.at[1], (partner, s)),
    ]
    for copy in shifts:
        copy.start()

    zero = jnp.zeros((RIM, C), jnp.float32)
    Ub[0:RIM, :] = zero
    Ub[BASE + R + RIM : BASE + R + 2 * RIM, :] = zero
    W1[0:RIM, :] = zero
    W1[BASE + R + RIM : BASE + R + 2 * RIM, :] = zero

    @pl.when(jnp.logical_not(has_up))
    def _():
        Ub[BASE - RIM : BASE, :] = zero
        Vb[BASE - RIM : BASE, :] = zero
        Pb[BASE - RIM : BASE, :] = zero + 1.0
        Cb[0, BASE - RIM : BASE, :] = zero
        Cb[1, BASE - RIM : BASE, :] = zero

    @pl.when(jnp.logical_not(has_down))
    def _():
        Ub[BASE + R : BASE + R + RIM, :] = zero
        Vb[BASE + R : BASE + R + RIM, :] = zero
        Pb[BASE + R : BASE + R + RIM, :] = zero + 1.0
        Cb[0, BASE + R : BASE + R + RIM, :] = zero
        Cb[1, BASE + R : BASE + R + RIM, :] = zero

    def chunk(idx):
        return (
            pl.ds(pl.multiple_of((idx // cpr) * 8, 8), 8),
            pl.ds(pl.multiple_of((idx % cpr) * W, 128), W),
        )

    for copy in loads[3:]:
        copy.wait()
    first = step0[0]
    cosines = [
        jnp.cos(
            jnp.float32(2.0 * jnp.pi / PERIOD)
            * jnp.full((8, 128), first + level, jnp.int32).astype(jnp.float32)
        )
        for level in range(STEPS)
    ]

    def depth_of(row):
        row = jnp.clip(row // TILE, 0, tile_rows - 1)
        return [mod[tmap[row, t]] for t in range(C // TILE)]

    def factors(depths):
        return [
            jnp.concatenate([1.0 + depth * cosines[level] for depth in depths], axis=1)
            for level in range(STEPS)
        ]

    first_row = s * R
    main_f = factors(depth_of(first_row))
    for copy in loads[:3]:
        copy.wait()

    def coefficients(base, fs):
        for level in range(STEPS):
            Q[level, base : base + 8, :] = time_step / (Pb[base : base + 8, :] * fs[level])

    for base in range(BASE, BASE + R, 8):
        coefficients(base, main_f)

    def first_step(base, keep):
        forcing = laplacian(Ub, base) - damping_rate * Vb[base : base + 8, :]
        speed = Vb[base : base + 8, :] + Q[0, base : base + 8, :] * forcing
        place = Ub[base : base + 8, :] + time_step * speed
        if keep is not None:
            place = place * keep
        Fo[0, base : base + 8, :] = forcing
        B1[base : base + 8, :] = speed
        U1[base : base + 8, :] = place

    for base in range(BASE + 8, BASE + R - 8, 8):
        first_step(base, None)

    @pl.when(j == 0)
    def _():
        own_rate.wait()

    @pl.when(j == 1)
    def _():
        rate_pair.wait_recv()

    rate_next[0].wait_recv()
    for b in range(0, H, 8):
        own = jnp.exp(-R0[b : b + 8, :] / n)
        R0[b : b + 8, :] = own
        entering = jnp.exp(-R1[b : b + 8, :] / n)
        R1[b : b + 8, :] = entering
        Am[b : b + 8, :] = own * entering
    a_copies = []
    for d in range(1, nc):
        to = lax.rem(c + d, nc)
        rows, cols = chunk(to)
        copy = remote(Am.at[rows, cols], RA.at[d], a_s.at[d], a_r.at[d], (2 * to + j, s))
        copy.start()
        a_copies.append(copy)

    @pl.when(has_down)
    def _():
        for copy in up_halo:
            copy.wait_recv()

    @pl.when(has_up)
    def _():
        for copy in down_halo:
            copy.wait_recv()

    coefficients(BASE - RIM, factors(depth_of(first_row - 1)))
    coefficients(BASE + R, factors(depth_of(first_row + R)))
    keep_top = has_up.astype(jnp.float32)
    keep_bottom = has_down.astype(jnp.float32)
    first_step(BASE - RIM, keep_top)
    first_step(BASE, None)
    first_step(BASE + R - 8, None)
    first_step(BASE + R, keep_bottom)

    for base in range(BASE, BASE + R, 8):
        r = base - BASE
        forcing = laplacian(U1, base) - damping_rate * B1[base : base + 8, :]
        speed = B1[base : base + 8, :] + Q[1, base : base + 8, :] * forcing
        place = U1[base : base + 8, :] + time_step * speed
        Fo[1, base : base + 8, :] = forcing
        ends[0, r : r + 8, :] = place
        ends[1, r : r + 8, :] = speed

    m_copy = remote(ends.at[:, other], Mp, m_s, m_r, (partner, s))
    m_copy.start()
    for copy in shifts:
        copy.wait_recv()
    m_copy.wait_recv()

    def main_half(b):
        return pl.ds(pl.multiple_of(BASE + j * H + b, 8), 8)

    starts = (Ub, Vb)

    @pl.when(j == 0)
    def _():
        for b in range(0, H, 8):
            entering = R1[b : b + 8, :]
            for f in range(2):
                term = (
                    ends[f, b : b + 8, :] - Fp[f, b : b + 8, :] + R0[b : b + 8, :] * Mp[f, b : b + 8, :]
                )
                Ep[f, b : b + 8, :] = term
                E[f, b : b + 8, :] = entering * term - starts[f][BASE + b : BASE + b + 8, :]

    @pl.when(j == 1)
    def _():
        for b in range(0, H, 8):
            entering = R1[b : b + 8, :]
            for f in range(2):
                term = (
                    Mp[f, b : b + 8, :]
                    - starts[f][BASE + H + b : BASE + H + b + 8, :]
                    + R0[b : b + 8, :] * ends[f, H + b : H + b + 8, :]
                )
                Ep[f, b : b + 8, :] = term
                E[f, b : b + 8, :] = entering * term - Fp[f, b : b + 8, :]

    e_copies = []
    for d in range(1, nc):
        to = lax.rem(c + d, nc)
        rows, cols = chunk(to)
        copy = remote(E.at[:, rows, cols], RE.at[d], e_s.at[d], e_r.at[d], (2 * to + j, s))
        copy.start()
        e_copies.append(copy)

    rows, cols = chunk(c)
    for copy in a_copies:
        copy.wait_recv()
    for copy in e_copies:
        copy.wait_recv()
    a0 = Am[rows, cols]
    total = a0
    state = [RE[1, f] for f in range(2)]
    total = total * RA[1]
    for d in range(2, nc):
        total = total * RA[d]
        state = [RA[d] * state[f] + RE[d, f] for f in range(2)]
    below = 1.0 / (1.0 - total)
    state = [(a0 * state[f] + E[f, rows, cols]) * below for f in range(2)]
    g_copies = []
    for d in range(1, nc):
        for f in range(2):
            X[d, f] = state[f]
        to = lax.rem(c - d + nc, nc)
        copy = remote(X.at[d], G.at[:, rows, cols], g_s.at[d], g_r.at[d], (2 * to + j, s))
        copy.start()
        g_copies.append(copy)
        state = [RA[d] * state[f] + RE[d, f] for f in range(2)]
    for f in range(2):
        G[f, rows, cols] = state[f]
    for copy in g_copies:
        copy.wait_recv()

    @pl.when(j == 0)
    def _():
        for b in range(0, H, 8):
            for f in range(2):
                value = G[f, b : b + 8, :]
                Cx[f, b : b + 8, :] = value + Mp[f, b : b + 8, :]
                Cb[f, BASE + b : BASE + b + 8, :] = R0[b : b + 8, :] * value + Ep[f, b : b + 8, :]

    @pl.when(j == 1)
    def _():
        for b in range(0, H, 8):
            for f in range(2):
                value = G[f, b : b + 8, :]
                early = R0[b : b + 8, :] * value + Ep[f, b : b + 8, :]
                Cb[f, BASE + H + b : BASE + H + b + 8, :] = value + ends[f, H + b : H + b + 8, :]
                Cx[f, b : b + 8, :] = early
                Pre[f, H + b : H + b + 8, :] = early

    main_mine = pl.ds(pl.multiple_of(BASE + j * H, 8), H)
    edge_cx = pl.ds(pl.multiple_of(j * (H - RIM), 8), RIM)
    edge_cb = pl.ds(pl.multiple_of(BASE + j * (R - RIM), 8), RIM)
    far = pl.ds(pl.multiple_of((1 - j) * (R + RIM) + BASE - RIM, 8), RIM)
    nb = lax.rem(s + 2 * j - 1 + S, S)
    c_copy = remote(Cx, Cb.at[:, main_mine], c_s, c_r, (partner, s))
    h_own = remote(Cb.at[:, edge_cb], Cb.at[:, far], h_s.at[0], h_r.at[j], (k, nb))
    h_par = remote(Cx.at[:, edge_cx], Cb.at[:, far], h_s.at[1], h_r.at[j], (partner, nb))
    sends_halo = jnp.where(j == 0, has_up.astype(jnp.int32), has_down.astype(jnp.int32)) == 1

    @pl.when(sends_halo)
    def _():
        h_own.start()
        h_par.start()

    c_copy.start()
    p_low = remote(Cx, Pre.at[:, low], p_s.at[0], p_r.at[0], (2 * c_next, s))
    p_pair = remote(Cb.at[:, main_mine], Pre.at[:, low], p_s.at[1], p_r.at[0], (partner, s))
    p_high = remote(Cb.at[:, main_mine], Pre.at[:, high], p_s.at[0], p_r.at[1], (2 * c_next, s))

    @pl.when(j == 0)
    def _():
        p_low.start()
        p_pair.start()

    @pl.when(j == 1)
    def _():
        p_high.start()

    c_copy.wait_recv()

    acc = jnp.zeros((8, C), jnp.float32)
    cos_cols = [jnp.concatenate([cosine] * (C // TILE), axis=1) for cosine in cosines]

    def weigh(base):
        total_v = Cb[1, base : base + 8, :] + time_step * Cb[0, base : base + 8, :]
        q = Q[1, base : base + 8, :]
        W1[base : base + 8, :] = q * total_v
        B1[base : base + 8, :] = (1.0 - damping_rate * q) * total_v
        return total_v, q

    for base in range(BASE, BASE + R, 8):
        total_v, q = weigh(base)
        acc = acc + Pb[base : base + 8, :] * cos_cols[1] * total_v * Fo[1, base : base + 8, :] * (q * q)

    def second(base, keep):
        back_u = Cb[0, base : base + 8, :] + laplacian(W1, base)
        total_v = B1[base : base + 8, :] + time_step * back_u
        q = Q[0, base : base + 8, :]
        weighted = q * total_v
        if keep is not None:
            weighted = weighted * keep
        W0[base : base + 8, :] = weighted
        return back_u, total_v, q

    def inner(base):
        back_u, total_v, q = second(base, None)
        U1[base : base + 8, :] = back_u
        B1[base : base + 8, :] = (1.0 - damping_rate * q) * total_v
        return Pb[base : base + 8, :] * cos_cols[0] * total_v * Fo[0, base : base + 8, :] * (q * q)

    for base in range(BASE + 8, BASE + R - 8, 8):
        acc = acc + inner(base)

    @pl.when(has_up)
    def _():
        remote(Cb.at[:, edge_cb], Cb.at[:, tops], h_s.at[0], h_r.at[1], (k, nb)).wait_recv()

    @pl.when(has_down)
    def _():
        remote(Cb.at[:, edge_cb], Cb.at[:, bottoms], h_s.at[0], h_r.at[0], (k, nb)).wait_recv()

    weigh(BASE - RIM)
    weigh(BASE + R)
    second(BASE - RIM, keep_top)
    second(BASE + R, keep_bottom)
    acc = acc + inner(BASE)
    acc = acc + inner(BASE + R - 8)

    lane = lax.broadcasted_iota(jnp.int32, (8, 128), 1)
    tile_row = first_row // TILE
    share = jnp.zeros((8, 128), jnp.float32)
    for t in range(C // TILE):
        summed = jnp.sum(acc[:, t * TILE : (t + 1) * TILE], axis=1, keepdims=True)
        share = share + jnp.where(lane == tmap[tile_row, t], summed, 0.0)
    part[0] = share * (-1.0 / time_step)
    d1 = []
    for d in range(1, nc):
        copy = remote(part.at[0], gat1.at[d], d1_s.at[d], d1_r.at[d], (chip(d), s))
        copy.start()
        d1.append(copy)

    for base in range(BASE, BASE + R, 8):
        U1[base : base + 8, :] = U1[base : base + 8, :] + laplacian(W0, base)

    for copy in d1:
        copy.wait_recv()
    share = part[0]
    for d in range(1, nc):
        share = share + gat1[d]
    part[1] = share
    d2 = []
    for d in range(1, 2 * S):
        at = lax.rem(s * 2 + j + d, 2 * S)
        copy = remote(part.at[1], gat2.at[d], d2_s.at[d], d2_r.at[d], (2 * c + at % 2, at // 2))
        copy.start()
        d2.append(copy)
    p_low.wait_recv()

    @pl.when(j == 0)
    def _():
        p_high.wait_recv()

    for base in range(BASE, BASE + R, 8):
        r = base - BASE
        out_u[r : r + 8, :] = U1[base : base + 8, :] - Pre[0, r : r + 8, :]
        out_v[r : r + 8, :] = B1[base : base + 8, :] - Pre[1, r : r + 8, :]
    for copy in d2:
        copy.wait_recv()
    for d in range(1, 2 * S):
        share = share + gat2[d]
    out_g[...] = jnp.sum(share, axis=0, keepdims=True)

    @pl.when(has_up)
    def _():
        for copy in up_halo:
            copy.wait_send()

    @pl.when(has_down)
    def _():
        for copy in down_halo:
            copy.wait_send()

    @pl.when(sends_halo)
    def _():
        h_own.wait_send()
        h_par.wait_send()

    @pl.when(j == 0)
    def _():
        rate_pair.wait_send()
        p_low.wait_send()
        p_pair.wait_send()

    @pl.when(j == 1)
    def _():
        for copy in [*rate_next, p_high]:
            copy.wait_send()

    for copy in [*shifts, *a_copies, m_copy, *e_copies, *g_copies, c_copy, *d1, *d2]:
        copy.wait_send()


def store_outputs(u, v, g, out_u, out_v, out_g):
    out_u[...] = u[...]
    out_v[...] = v[...]
    out_g[...] = g[...]


def solution(mesh):
    n = mesh.shape["tm"]
    S = mesh.shape["strip"]
    nc = n // 2

    def shards(forward_u, forward_v, permittivity, coarse_rate, modulation, tile_map, start_step):
        R, C = permittivity.shape
        H = R // 2
        W = H * C // (8 * nc)
        assert TILE % R == 0 and W % 128 == 0 and C % W == 0
        f32 = jnp.float32
        ext = R + 2 * BASE
        vmem = lambda *shape: pltpu.VMEM(shape, f32)
        dma = lambda *shape: pltpu.SemaphoreType.DMA(shape)
        any_spec = pl.BlockSpec(memory_space=pl.ANY)
        hbm = pl.BlockSpec(memory_space=pltpu.HBM)
        whole = pl.BlockSpec(memory_space=pltpu.VMEM)
        operands = (
            forward_u[0], forward_v[0], permittivity, coarse_rate[0], modulation, tile_map, start_step
        )
        out_u, out_v, out_g = pl.pallas_call(
            functools.partial(kernel, n, S, tile_map.shape[0]),
            out_shape=(
                jax.ShapeDtypeStruct((R, C), f32),
                jax.ShapeDtypeStruct((R, C), f32),
                jax.ShapeDtypeStruct((1, 128), f32),
            ),
            in_specs=[hbm] * 7,
            out_specs=(whole, whole, whole),
            scratch_shapes=[
                vmem(ext, C), vmem(ext, C), vmem(ext, C), vmem(2, ext, C), vmem(2, ext, C),
                vmem(ext, C), vmem(2, ext, C), vmem(ext, C), vmem(ext, C), vmem(ext, C),
                vmem(2, H, C), vmem(2, R, C), vmem(H, C), vmem(H, C), vmem(H, C),
                vmem(2, H, C), vmem(2, H, C), vmem(2, H, C), vmem(nc, 8, W), vmem(nc, 2, 8, W),
                vmem(nc, 2, 8, W), vmem(2, H, C), vmem(2, H, C), vmem(2, R, C),
                vmem(2, 8, 128), vmem(nc, 8, 128), vmem(2 * S, 8, 128),
                pltpu.SMEM(modulation.shape, f32), pltpu.SMEM(tile_map.shape, jnp.int32),
                pltpu.SMEM(start_step.shape, jnp.int32),
                dma(7), dma(2, 3), dma(2, 3), dma(2), dma(2), dma(2), dma(2), dma(nc), dma(nc),
                dma(), dma(), dma(nc), dma(nc), dma(nc), dma(nc), dma(), dma(), dma(2), dma(2),
                dma(2), dma(2), dma(nc), dma(nc), dma(2 * S), dma(2 * S),
            ],
            compiler_params=pltpu.CompilerParams(
                collective_id=0, has_side_effects=True, vmem_limit_bytes=48 * 1024 * 1024
            ),
        )(*[pltpu.with_memory_space_constraint(a, pltpu.HBM) for a in operands[:6]], operands[6])
        out_u, out_v, out_g = pl.pallas_call(
            store_outputs,
            out_shape=(
                jax.ShapeDtypeStruct((R, C), f32),
                jax.ShapeDtypeStruct((R, C), f32),
                jax.ShapeDtypeStruct((1, 128), f32),
            ),
            in_specs=[whole] * 3,
            out_specs=(whole,) * 3,
            compiler_params=pltpu.CompilerParams(vmem_limit_bytes=8*1024*1024),
        )(out_u, out_v, out_g)
        return out_u[None], out_v[None], out_g[0, : modulation.shape[0]]

    placed = (
        P("tm", "strip", None),
        P("tm", "strip", None),
        P("strip", None),
        P("tm", "strip", None),
        P(),
        P(),
        P("tm"),
    )
    return jax.shard_map(
        shards,
        mesh=mesh,
        in_specs=placed,
        out_specs=(P("tm", "strip", None), P("tm", "strip", None), P()),
        check_vma=False,
    )
```

```python
import functools

import jax
import jax.numpy as jnp
from jax import lax
from jax.experimental import pallas as pl
from jax.experimental.pallas import tpu as pltpu
from jax.sharding import PartitionSpec as P

TILE = 128
STEPS = 2
STENCIL = 4
PERIOD = 256
RIM = STEPS * STENCIL
BASE = 2 * RIM

stencil_coef = (-205.0 / 72.0, 8.0 / 5.0, -1.0 / 5.0, 8.0 / 315.0, -1.0 / 560.0)
time_step = 0.4
damping_rate = 0.1

MESH = pl.DeviceIdType.MESH


def laplacian(ref, base):
    center = ref[base : base + 8, :]
    cols = center.shape[1]
    summed = (2.0 * stencil_coef[0]) * center
    for o in range(1, STENCIL + 1):
        along_x = ref[base + o : base + o + 8, :] + ref[base - o : base - o + 8, :]
        along_y = pltpu.roll(center, o, 1) + pltpu.roll(center, cols - o, 1)
        summed = summed + stencil_coef[o] * (along_x + along_y)
    return summed


def kernel(
    n, S, tile_rows,
    u_in, v_in, p_in, rate_in, mod_in, tmap_in, step_in,
    out_u, out_v, out_g,
    Ub, Vb, Pb, Q, Fo, U1, Cb, W1, B1, W0, Fp, ends, R0, R1, Am, Mp, Ep, E, RA, RE, X, G, Cx, Pre,
    part, gat1, gat2, mod, tmap, step0,
    load_sem, halo_s, halo_r, shift_s, shift_r, rate_s, rate_r, a_s, a_r, m_s, m_r, e_s, e_r,
    g_s, g_r, c_s, c_r, h_s, h_r, p_s, p_r, d1_s, d1_r, d2_s, d2_r,
):
    k = lax.axis_index("tm")
    s = lax.axis_index("strip")
    nc = n // 2
    c = k // 2
    j = k % 2
    partner = 2 * c + 1 - j
    R, C = out_u.shape
    H = R // 2
    W = H * C // (8 * nc)
    cpr = C // W

    turns = sorted(range(1, nc), key=lambda d: (-min(d, nc - d), d))

    def chip(d):
        return 2 * lax.rem(c + d + nc, nc) + j

    mine = pl.ds(pl.multiple_of(j * H, 8), H)
    other = pl.ds(pl.multiple_of((1 - j) * H, 8), H)
    loads = [
        pltpu.make_async_copy(u_in, Ub.at[pl.ds(BASE, R)], load_sem.at[0]),
        pltpu.make_async_copy(v_in, Vb.at[pl.ds(BASE, R)], load_sem.at[1]),
        pltpu.make_async_copy(p_in, Pb.at[pl.ds(BASE, R)], load_sem.at[2]),
        pltpu.make_async_copy(mod_in, mod, load_sem.at[4]),
        pltpu.make_async_copy(tmap_in, tmap, load_sem.at[5]),
        pltpu.make_async_copy(step_in, step0, load_sem.at[6]),
    ]
    for load in loads:
        load.start()

    own_rate = pltpu.make_async_copy(rate_in.at[pl.ds(0, H)], R0, load_sem.at[3])

    @pl.when(j == 0)
    def _():
        own_rate.start()

    barrier = pltpu.get_barrier_semaphore()
    for d in range(1, nc):
        pl.semaphore_signal(barrier, inc=1, device_id=(chip(d), s), device_id_type=MESH)
    for d in range(1, 2 * S):
        at = lax.rem(s * 2 + j + d, 2 * S)
        pl.semaphore_signal(
            barrier, inc=1, device_id=(2 * c + at % 2, at // 2), device_id_type=MESH
        )
    aside = lax.rem(k + 2 * j - 1 + n, n)
    pl.semaphore_signal(barrier, inc=1, device_id=(aside, s), device_id_type=MESH)
    pl.semaphore_wait(barrier, (nc - 1) + (2 * S - 1) + 1)

    def remote(src, dst, ss, rs, where):
        return pltpu.make_async_remote_copy(
            src_ref=src, dst_ref=dst, send_sem=ss, recv_sem=rs,
            device_id=where, device_id_type=MESH,
        )

    up = lax.rem(s + S - 1, S)
    down = lax.rem(s + 1, S)
    tops = pl.ds(BASE - RIM, RIM)
    bottoms = pl.ds(BASE + R, RIM)
    has_up = s > 0
    has_down = s < S - 1
    fields = ((u_in, Ub), (v_in, Vb), (p_in, Pb))
    up_halo = [
        remote(a.at[pl.ds(0, RIM)], b.at[bottoms], halo_s.at[0, i], halo_r.at[0, i], (k, up))
        for i, (a, b) in enumerate(fields)
    ]
    down_halo = [
        remote(a.at[pl.ds(R - RIM, RIM)], b.at[tops], halo_s.at[1, i], halo_r.at[1, i], (k, down))
        for i, (a, b) in enumerate(fields)
    ]

    @pl.when(has_up)
    def _():
        for copy in up_halo:
            copy.start()

    @pl.when(has_down)
    def _():
        for copy in down_halo:
            copy.start()

    low = pl.ds(0, H)
    high = pl.ds(H, H)
    c_next = lax.rem(c + 1, nc)
    rate_pair = remote(rate_in.at[high], R0, rate_s.at[0], rate_r.at[0], (partner, s))
    rate_next = [
        remote(rate_in.at[low], R1, rate_s.at[0], rate_r.at[1], (2 * c_next, s)),
        remote(rate_in.at[high], R1, rate_s.at[1], rate_r.at[1], (2 * c_next + 1, s)),
    ]

    @pl.when(j == 0)
    def _():
        rate_pair.start()

    @pl.when(j == 1)
    def _():
        for copy in rate_next:
            copy.start()

    shifts = [
        remote(u_in.at[other], Fp.at[0], shift_s.at[0], shift_r.at[0], (partner, s)),
        remote(v_in.at[other], Fp.at[1], shift_s.at[1], shift_r.at[1], (partner, s)),
    ]
    for copy in shifts:
        copy.start()

    zero = jnp.zeros((RIM, C), jnp.float32)
    Ub[0:RIM, :] = zero
    Ub[BASE + R + RIM : BASE + R + 2 * RIM, :] = zero
    W1[0:RIM, :] = zero
    W1[BASE + R + RIM : BASE + R + 2 * RIM, :] = zero

    @pl.when(jnp.logical_not(has_up))
    def _():
        Ub[BASE - RIM : BASE, :] = zero
        Vb[BASE - RIM : BASE, :] = zero
        Pb[BASE - RIM : BASE, :] = zero + 1.0
        Cb[0, BASE - RIM : BASE, :] = zero
        Cb[1, BASE - RIM : BASE, :] = zero

    @pl.when(jnp.logical_not(has_down))
    def _():
        Ub[BASE + R : BASE + R + RIM, :] = zero
        Vb[BASE + R : BASE + R + RIM, :] = zero
        Pb[BASE + R : BASE + R + RIM, :] = zero + 1.0
        Cb[0, BASE + R : BASE + R + RIM, :] = zero
        Cb[1, BASE + R : BASE + R + RIM, :] = zero

    def chunk(idx):
        return (
            pl.ds(pl.multiple_of((idx // cpr) * 8, 8), 8),
            pl.ds(pl.multiple_of((idx % cpr) * W, 128), W),
        )

    for copy in loads[3:]:
        copy.wait()
    first = step0[0]
    cosines = [
        jnp.cos(
            jnp.float32(2.0 * jnp.pi / PERIOD)
            * jnp.full((8, 128), first + level, jnp.int32).astype(jnp.float32)
        )
        for level in range(STEPS)
    ]

    def depth_of(row):
        row = jnp.clip(row // TILE, 0, tile_rows - 1)
        return [mod[tmap[row, t]] for t in range(C // TILE)]

    def factors(depths):
        return [
            jnp.concatenate([1.0 + depth * cosines[level] for depth in depths], axis=1)
            for level in range(STEPS)
        ]

    first_row = s * R
    main_f = factors(depth_of(first_row))
    for copy in loads[:3]:
        copy.wait()

    def coefficients(base, fs):
        for level in range(STEPS):
            Q[level, base : base + 8, :] = time_step / (Pb[base : base + 8, :] * fs[level])

    for base in range(BASE, BASE + R, 8):
        coefficients(base, main_f)

    def first_step(base, keep):
        forcing = laplacian(Ub, base) - damping_rate * Vb[base : base + 8, :]
        speed = Vb[base : base + 8, :] + Q[0, base : base + 8, :] * forcing
        place = Ub[base : base + 8, :] + time_step * speed
        if keep is not None:
            place = place * keep
        Fo[0, base : base + 8, :] = forcing
        B1[base : base + 8, :] = speed
        U1[base : base + 8, :] = place

    for base in range(BASE + 8, BASE + R - 8, 8):
        first_step(base, None)

    @pl.when(j == 0)
    def _():
        own_rate.wait()

    @pl.when(j == 1)
    def _():
        rate_pair.wait_recv()

    rate_next[0].wait_recv()
    for b in range(0, H, 8):
        own = jnp.exp(-R0[b : b + 8, :] / n)
        R0[b : b + 8, :] = own
        entering = jnp.exp(-R1[b : b + 8, :] / n)
        R1[b : b + 8, :] = entering
        Am[b : b + 8, :] = own * entering
    a_copies = []
    for d in turns:
        to = lax.rem(c + d, nc)
        rows, cols = chunk(to)
        copy = remote(Am.at[rows, cols], RA.at[d], a_s.at[d], a_r.at[d], (2 * to + j, s))
        copy.start()
        a_copies.append(copy)

    @pl.when(has_down)
    def _():
        for copy in up_halo:
            copy.wait_recv()

    @pl.when(has_up)
    def _():
        for copy in down_halo:
            copy.wait_recv()

    coefficients(BASE - RIM, factors(depth_of(first_row - 1)))
    coefficients(BASE + R, factors(depth_of(first_row + R)))
    keep_top = has_up.astype(jnp.float32)
    keep_bottom = has_down.astype(jnp.float32)
    first_step(BASE - RIM, keep_top)
    first_step(BASE, None)
    first_step(BASE + R - 8, None)
    first_step(BASE + R, keep_bottom)

    for base in range(BASE, BASE + R, 8):
        r = base - BASE
        forcing = laplacian(U1, base) - damping_rate * B1[base : base + 8, :]
        speed = B1[base : base + 8, :] + Q[1, base : base + 8, :] * forcing
        place = U1[base : base + 8, :] + time_step * speed
        Fo[1, base : base + 8, :] = forcing
        ends[0, r : r + 8, :] = place
        ends[1, r : r + 8, :] = speed

    m_copy = remote(ends.at[:, other], Mp, m_s, m_r, (partner, s))
    m_copy.start()
    for copy in shifts:
        copy.wait_recv()
    m_copy.wait_recv()

    def main_half(b):
        return pl.ds(pl.multiple_of(BASE + j * H + b, 8), 8)

    starts = (Ub, Vb)

    @pl.when(j == 0)
    def _():
        for b in range(0, H, 8):
            entering = R1[b : b + 8, :]
            for f in range(2):
                term = (
                    ends[f, b : b + 8, :] - Fp[f, b : b + 8, :] + R0[b : b + 8, :] * Mp[f, b : b + 8, :]
                )
                Ep[f, b : b + 8, :] = term
                E[f, b : b + 8, :] = entering * term - starts[f][BASE + b : BASE + b + 8, :]

    @pl.when(j == 1)
    def _():
        for b in range(0, H, 8):
            entering = R1[b : b + 8, :]
            for f in range(2):
                term = (
                    Mp[f, b : b + 8, :]
                    - starts[f][BASE + H + b : BASE + H + b + 8, :]
                    + R0[b : b + 8, :] * ends[f, H + b : H + b + 8, :]
                )
                Ep[f, b : b + 8, :] = term
                E[f, b : b + 8, :] = entering * term - Fp[f, b : b + 8, :]

    e_copies = []
    for d in turns:
        to = lax.rem(c + d, nc)
        rows, cols = chunk(to)
        copy = remote(E.at[:, rows, cols], RE.at[d], e_s.at[d], e_r.at[d], (2 * to + j, s))
        copy.start()
        e_copies.append(copy)

    rows, cols = chunk(c)
    for copy in a_copies:
        copy.wait_recv()
    for copy in e_copies:
        copy.wait_recv()
    a0 = Am[rows, cols]
    total = a0
    state = [RE[1, f] for f in range(2)]
    total = total * RA[1]
    for d in range(2, nc):
        total = total * RA[d]
        state = [RA[d] * state[f] + RE[d, f] for f in range(2)]
    below = 1.0 / (1.0 - total)
    state = [(a0 * state[f] + E[f, rows, cols]) * below for f in range(2)]
    g_copies = []
    for d in range(1, nc):
        for f in range(2):
            X[d, f] = state[f]
        to = lax.rem(c - d + nc, nc)
        copy = remote(X.at[d], G.at[:, rows, cols], g_s.at[d], g_r.at[d], (2 * to + j, s))
        copy.start()
        g_copies.append(copy)
        state = [RA[d] * state[f] + RE[d, f] for f in range(2)]
    for f in range(2):
        G[f, rows, cols] = state[f]
    for copy in g_copies:
        copy.wait_recv()

    @pl.when(j == 0)
    def _():
        for b in range(0, H, 8):
            for f in range(2):
                value = G[f, b : b + 8, :]
                Cx[f, b : b + 8, :] = value + Mp[f, b : b + 8, :]
                Cb[f, BASE + b : BASE + b + 8, :] = R0[b : b + 8, :] * value + Ep[f, b : b + 8, :]

    @pl.when(j == 1)
    def _():
        for b in range(0, H, 8):
            for f in range(2):
                value = G[f, b : b + 8, :]
                early = R0[b : b + 8, :] * value + Ep[f, b : b + 8, :]
                Cb[f, BASE + H + b : BASE + H + b + 8, :] = value + ends[f, H + b : H + b + 8, :]
                Cx[f, b : b + 8, :] = early
                Pre[f, H + b : H + b + 8, :] = early

    main_mine = pl.ds(pl.multiple_of(BASE + j * H, 8), H)
    edge_cx = pl.ds(pl.multiple_of(j * (H - RIM), 8), RIM)
    edge_cb = pl.ds(pl.multiple_of(BASE + j * (R - RIM), 8), RIM)
    far = pl.ds(pl.multiple_of((1 - j) * (R + RIM) + BASE - RIM, 8), RIM)
    nb = lax.rem(s + 2 * j - 1 + S, S)
    c_copy = remote(Cx, Cb.at[:, main_mine], c_s, c_r, (partner, s))
    h_own = remote(Cb.at[:, edge_cb], Cb.at[:, far], h_s.at[0], h_r.at[j], (k, nb))
    h_par = remote(Cx.at[:, edge_cx], Cb.at[:, far], h_s.at[1], h_r.at[j], (partner, nb))
    sends_halo = jnp.where(j == 0, has_up.astype(jnp.int32), has_down.astype(jnp.int32)) == 1

    @pl.when(sends_halo)
    def _():
        h_own.start()
        h_par.start()

    c_copy.start()
    p_low = remote(Cx, Pre.at[:, low], p_s.at[0], p_r.at[0], (2 * c_next, s))
    p_pair = remote(Cb.at[:, main_mine], Pre.at[:, low], p_s.at[1], p_r.at[0], (partner, s))
    p_high = remote(Cb.at[:, main_mine], Pre.at[:, high], p_s.at[0], p_r.at[1], (2 * c_next, s))

    @pl.when(j == 0)
    def _():
        p_low.start()
        p_pair.start()

    @pl.when(j == 1)
    def _():
        p_high.start()

    c_copy.wait_recv()

    acc = jnp.zeros((8, C), jnp.float32)
    cos_cols = [jnp.concatenate([cosine] * (C // TILE), axis=1) for cosine in cosines]

    def weigh(base):
        total_v = Cb[1, base : base + 8, :] + time_step * Cb[0, base : base + 8, :]
        q = Q[1, base : base + 8, :]
        W1[base : base + 8, :] = q * total_v
        B1[base : base + 8, :] = (1.0 - damping_rate * q) * total_v
        return total_v, q

    for base in range(BASE, BASE + R, 8):
        total_v, q = weigh(base)
        acc = acc + Pb[base : base + 8, :] * cos_cols[1] * total_v * Fo[1, base : base + 8, :] * (q * q)

    def second(base, keep):
        back_u = Cb[0, base : base + 8, :] + laplacian(W1, base)
        total_v = B1[base : base + 8, :] + time_step * back_u
        q = Q[0, base : base + 8, :]
        weighted = q * total_v
        if keep is not None:
            weighted = weighted * keep
        W0[base : base + 8, :] = weighted
        return back_u, total_v, q

    def inner(base):
        back_u, total_v, q = second(base, None)
        U1[base : base + 8, :] = back_u
        B1[base : base + 8, :] = (1.0 - damping_rate * q) * total_v
        return Pb[base : base + 8, :] * cos_cols[0] * total_v * Fo[0, base : base + 8, :] * (q * q)

    for base in range(BASE + 8, BASE + R - 8, 8):
        acc = acc + inner(base)

    @pl.when(has_up)
    def _():
        remote(Cb.at[:, edge_cb], Cb.at[:, tops], h_s.at[0], h_r.at[1], (k, nb)).wait_recv()

    @pl.when(has_down)
    def _():
        remote(Cb.at[:, edge_cb], Cb.at[:, bottoms], h_s.at[0], h_r.at[0], (k, nb)).wait_recv()

    weigh(BASE - RIM)
    weigh(BASE + R)
    second(BASE - RIM, keep_top)
    second(BASE + R, keep_bottom)
    acc = acc + inner(BASE)
    acc = acc + inner(BASE + R - 8)

    lane = lax.broadcasted_iota(jnp.int32, (8, 128), 1)
    tile_row = first_row // TILE
    share = jnp.zeros((8, 128), jnp.float32)
    for t in range(C // TILE):
        summed = jnp.sum(acc[:, t * TILE : (t + 1) * TILE], axis=1, keepdims=True)
        share = share + jnp.where(lane == tmap[tile_row, t], summed, 0.0)
    part[0] = share * (-1.0 / time_step)
    d1 = []
    for d in range(1, nc):
        copy = remote(part.at[0], gat1.at[d], d1_s.at[d], d1_r.at[d], (chip(d), s))
        copy.start()
        d1.append(copy)

    for base in range(BASE, BASE + R, 8):
        U1[base : base + 8, :] = U1[base : base + 8, :] + laplacian(W0, base)

    for copy in d1:
        copy.wait_recv()
    share = part[0]
    for d in range(1, nc):
        share = share + gat1[d]
    part[1] = share
    d2 = []
    for d in range(1, 2 * S):
        at = lax.rem(s * 2 + j + d, 2 * S)
        copy = remote(part.at[1], gat2.at[d], d2_s.at[d], d2_r.at[d], (2 * c + at % 2, at // 2))
        copy.start()
        d2.append(copy)
    p_low.wait_recv()

    @pl.when(j == 0)
    def _():
        p_high.wait_recv()

    for base in range(BASE, BASE + R, 8):
        r = base - BASE
        out_u[r : r + 8, :] = U1[base : base + 8, :] - Pre[0, r : r + 8, :]
        out_v[r : r + 8, :] = B1[base : base + 8, :] - Pre[1, r : r + 8, :]
    for copy in d2:
        copy.wait_recv()
    for d in range(1, 2 * S):
        share = share + gat2[d]
    out_g[...] = jnp.sum(share, axis=0, keepdims=True)

    @pl.when(has_up)
    def _():
        for copy in up_halo:
            copy.wait_send()

    @pl.when(has_down)
    def _():
        for copy in down_halo:
            copy.wait_send()

    @pl.when(sends_halo)
    def _():
        h_own.wait_send()
        h_par.wait_send()

    @pl.when(j == 0)
    def _():
        rate_pair.wait_send()
        p_low.wait_send()
        p_pair.wait_send()

    @pl.when(j == 1)
    def _():
        for copy in [*rate_next, p_high]:
            copy.wait_send()

    for copy in [*shifts, *a_copies, m_copy, *e_copies, *g_copies, c_copy, *d1, *d2]:
        copy.wait_send()


def store_outputs(u, v, g, out_u, out_v, out_g):
    out_u[...] = u[...]
    out_v[...] = v[...]
    out_g[...] = g[0, : out_g.shape[0]]


def solution(mesh):
    n = mesh.shape["tm"]
    S = mesh.shape["strip"]
    nc = n // 2

    def shards(forward_u, forward_v, permittivity, coarse_rate, modulation, tile_map, start_step):
        R, C = permittivity.shape
        H = R // 2
        W = H * C // (8 * nc)
        assert TILE % R == 0 and W % 128 == 0 and C % W == 0
        f32 = jnp.float32
        ext = R + 2 * BASE
        vmem = lambda *shape: pltpu.VMEM(shape, f32)
        dma = lambda *shape: pltpu.SemaphoreType.DMA(shape)
        any_spec = pl.BlockSpec(memory_space=pl.ANY)
        hbm = pl.BlockSpec(memory_space=pltpu.HBM)
        whole = pl.BlockSpec(memory_space=pltpu.VMEM)
        operands = (
            forward_u[0], forward_v[0], permittivity, coarse_rate[0], modulation, tile_map, start_step
        )
        out_u, out_v, out_g = pl.pallas_call(
            functools.partial(kernel, n, S, tile_map.shape[0]),
            out_shape=(
                jax.ShapeDtypeStruct((R, C), f32),
                jax.ShapeDtypeStruct((R, C), f32),
                jax.ShapeDtypeStruct((1, 128), f32),
            ),
            in_specs=[hbm] * 7,
            out_specs=(whole, whole, whole),
            scratch_shapes=[
                vmem(ext, C), vmem(ext, C), vmem(ext, C), vmem(2, ext, C), vmem(2, ext, C),
                vmem(ext, C), vmem(2, ext, C), vmem(ext, C), vmem(ext, C), vmem(ext, C),
                vmem(2, H, C), vmem(2, R, C), vmem(H, C), vmem(H, C), vmem(H, C),
                vmem(2, H, C), vmem(2, H, C), vmem(2, H, C), vmem(nc, 8, W), vmem(nc, 2, 8, W),
                vmem(nc, 2, 8, W), vmem(2, H, C), vmem(2, H, C), vmem(2, R, C),
                vmem(2, 8, 128), vmem(nc, 8, 128), vmem(2 * S, 8, 128),
                pltpu.SMEM(modulation.shape, f32), pltpu.SMEM(tile_map.shape, jnp.int32),
                pltpu.SMEM(start_step.shape, jnp.int32),
                dma(7), dma(2, 3), dma(2, 3), dma(2), dma(2), dma(2), dma(2), dma(nc), dma(nc),
                dma(), dma(), dma(nc), dma(nc), dma(nc), dma(nc), dma(), dma(), dma(2), dma(2),
                dma(2), dma(2), dma(nc), dma(nc), dma(2 * S), dma(2 * S),
            ],
            compiler_params=pltpu.CompilerParams(
                collective_id=0, has_side_effects=True, vmem_limit_bytes=48 * 1024 * 1024
            ),
        )(*[pltpu.with_memory_space_constraint(a, pltpu.HBM) for a in operands[:6]], operands[6])
        out_u, out_v, out_g = pl.pallas_call(
            store_outputs,
            out_shape=(
                jax.ShapeDtypeStruct((R, C), f32),
                jax.ShapeDtypeStruct((R, C), f32),
                jax.ShapeDtypeStruct(modulation.shape, f32),
            ),
            in_specs=[whole] * 3,
            out_specs=(whole,) * 3,
            compiler_params=pltpu.CompilerParams(vmem_limit_bytes=8*1024*1024),
        )(out_u, out_v, out_g)
        return out_u[None], out_v[None], out_g

    placed = (
        P("tm", "strip", None),
        P("tm", "strip", None),
        P("strip", None),
        P("tm", "strip", None),
        P(),
        P(),
        P("tm"),
    )
    return jax.shard_map(
        shards,
        mesh=mesh,
        in_specs=placed,
        out_specs=(P("tm", "strip", None), P("tm", "strip", None), P()),
        check_vma=False,
    )
```
